128 devices in a mesh: own: 4 (over x), seq: 8 (over z, y_hi), tp: 4 (over y_lo, core).
Axes of the slice: x: 4, y: 4 (y_hi: 2, y_lo: 2; y = y_hi * 2 + y_lo), z: 4, core: 2. Of those that a mesh axis runs over, the one named last changes fastest.
Arguments:
- latents: bfloat16 [1, 8192, 5120], P(None, ('own', 'seq')), may hold values from -6 to 6
- policy_out: bfloat16 [1, 8192, 5120], P(None, ('own', 'seq'), 'tp'), may hold values from -6 to 6
- w_qkv: bfloat16 [16, 5120, 3, 2560], P('own', 'seq', None, 'tp'), may hold values from -0.078125 to 0.078125
- w_out: bfloat16 [16, 2560, 5120], P('own', 'tp', 'seq'), may hold values from -0.125 to 0.125
- qk_gains: bfloat16 [16, 2, 2560], P('own', None, 'tp'), may hold values from 2 to 8
- mod_table: float32 [8, 3, 5120], replicated, may hold values from -3 to 3
- timestep: int32 [1], replicated, may hold values from 0 to 7
- owner: int32 [1], replicated, may hold values from 0 to 15
Outputs:
- block_out: bfloat16 [1, 8192, 5120], P(None, ('own', 'seq'), 'tp')
- sq_err: float32 [1, 8192], P(None, ('own', 'seq'))
The draws below stay inside these ranges and needn't reach their ends.
All inputs are finite; a program needn't handle non-finite values.
Results may differ from the reference program's by a relative error of at most 0.0069.
Values may be sent and summed in bfloat16 or wider, within the bound.
A program may use at most 192 MiB of HBM per device.

```python
import jax
import jax.numpy as jnp
from jax import lax

D = 5120
HEADS = 20
HD = 128
NSTEP = 8
LAYERS = 1
HW = 2560
SEQ_LEN = 8192
STORED = 16


def draw_qk_gains(key, part):
    key_base = jax.random.fold_in(key, 71)
    base = jax.random.uniform(key_base, (STORED, 2, HW), jnp.float32, 2.0, 2.9)
    gains = base
    return gains.astype(jnp.bfloat16)


def block_levels(key, extent, pieces, smallest, top_value):
    level, own = 1.0, jax.random.fold_in(key, 6)
    for position, blocks in pieces:
        heights = jnp.exp(jax.random.uniform(jax.random.fold_in(own, position), (blocks,), jnp.float32, smallest / len(pieces), top_value / len(pieces)))
        level = level * jnp.repeat(heights, extent[position] // blocks).reshape([-1 if axis == position else 1 for axis in range(len(extent))])
    return level


def noise(rng, shape, width, reach, shards=(), kind=jnp.bfloat16):
    loudness = block_levels(rng, shape, shards, -0.22, 0.18) if shards else 1.0
    values = jax.random.normal(rng, shape, jnp.float32) * width * loudness
    return jnp.minimum(jnp.maximum(values, -reach), reach).astype(kind)


def setup_inputs(seed: int = 0) -> dict:
    key_list = jax.random.split(jax.random.key(seed), 9)
    latents = noise(key_list[0], (1, SEQ_LEN, D), 1.0, 6.0, ((1, 32),))
    policy_out = noise(key_list[1], (1, SEQ_LEN, D), 1.0, 6.0, ((1, 32), (2, 4)))
    w_qkv = noise(key_list[2], (STORED, D, 3, HW), D ** -0.5, 0.078125, ((0, 4), (1, 8), (3, 4)))
    w_out = noise(key_list[3], (STORED, HW, D), HW ** -0.5, 0.125, ((0, 4), (1, 4), (2, 8)))
    qk_gains = draw_qk_gains(jax.random.fold_in(key_list[8], 71), 0)
    mod_table = noise(key_list[5], (NSTEP, 3, D), 0.5, 3.0, (), jnp.float32)
    timestep = jax.random.randint(key_list[6], (1,), 0, NSTEP).astype(jnp.int32)
    owner = jax.random.randint(key_list[7], (LAYERS,), 0, STORED).astype(jnp.int32)
    return dict(latents=latents, policy_out=policy_out, w_qkv=w_qkv, w_out=w_out, qk_gains=qk_gains, mod_table=mod_table, timestep=timestep, owner=owner)


def reference(latents, policy_out, w_qkv, w_out, qk_gains, mod_table, timestep, owner):
    root = owner[0]
    weights_qkv = lax.dynamic_index_in_dim(w_qkv, root, 0, keepdims=False)
    weights_out = lax.dynamic_index_in_dim(w_out, root, 0, keepdims=False)
    gains = lax.dynamic_index_in_dim(qk_gains, root, 0, keepdims=False).astype(jnp.float32)
    onehot = (jnp.arange(NSTEP, dtype=jnp.int32) == timestep[0]).astype(jnp.float32)
    modulation = jnp.tensordot(onehot, mod_table, axes=1, precision=lax.Precision.HIGHEST)
    shift, scale, gate = (modulation[0], modulation[1], modulation[2])
    inputs = latents[0].astype(jnp.float32)
    center = lax.optimization_barrier(jnp.mean(inputs, axis=-1, keepdims=True))
    spread = lax.optimization_barrier(jnp.mean((inputs - center) ** 2, axis=-1, keepdims=True))
    normed = (inputs - center) * lax.rsqrt(spread + 1e-06)
    modulated = (normed * (1.0 + scale) + shift).astype(jnp.bfloat16)
    qkv = jnp.dot(modulated, weights_qkv.reshape(D, 3 * HW), preferred_element_type=jnp.float32)
    qkv = qkv.reshape(SEQ_LEN, 3, HW)
    query, key, value = (qkv[:, 0], qkv[:, 1], qkv[:, 2])
    query = (query * lax.rsqrt(lax.optimization_barrier(jnp.mean(query * query, axis=-1, keepdims=True)) + 1e-06) * gains[0]).astype(jnp.bfloat16)
    key = (key * lax.rsqrt(lax.optimization_barrier(jnp.mean(key * key, axis=-1, keepdims=True)) + 1e-06) * gains[1]).astype(jnp.bfloat16)
    value = value.astype(jnp.bfloat16)
    query = query.reshape(SEQ_LEN, HEADS, HD).transpose(1, 0, 2)
    key = key.reshape(SEQ_LEN, HEADS, HD).transpose(1, 0, 2)
    value = value.reshape(SEQ_LEN, HEADS, HD).transpose(1, 0, 2)

    def one_head(triple):
        head_q, head_k, head_v = triple
        scores = jnp.dot(head_q, head_k.T, preferred_element_type=jnp.float32) * (1.0 / HD ** 0.5)
        probs = jnp.exp(scores - lax.optimization_barrier(jnp.max(scores, axis=-1, keepdims=True)))
        totals = lax.optimization_barrier(jnp.sum(probs, axis=-1, keepdims=True))
        mixed = jnp.dot(probs.astype(jnp.bfloat16), head_v, preferred_element_type=jnp.float32)
        return (mixed / totals).astype(jnp.bfloat16)
    attn = lax.map(one_head, (query, key, value))
    attn = attn.transpose(1, 0, 2).reshape(SEQ_LEN, HW)
    proj = jnp.dot(attn, weights_out, preferred_element_type=jnp.float32)
    block = (inputs + gate * proj).astype(jnp.bfloat16)
    differ = block.astype(jnp.float32) - policy_out[0].astype(jnp.float32)
    squares = lax.optimization_barrier(jnp.mean(differ * differ, axis=-1))
    return (block[None], squares[None])
```

```python
import jax
import jax.numpy as jnp
from jax import lax
from jax.experimental import pallas as pl
from jax.experimental.pallas import tpu as pltpu
from jax.sharding import PartitionSpec as P

D = 5120
HD = 128
HW = 2560
ROWS = 256
COLS = 640
HEADS_HERE = 5
QUARTER = 160
EPS = 1e-06
MESH = pl.DeviceIdType.MESH
ANY = pl.BlockSpec(memory_space=pl.ANY)
VMEM = pl.BlockSpec(memory_space=pltpu.VMEM)
LIMIT = 62 * 1024 * 1024


def remote(src, dst, send, recv, device):
    return pltpu.make_async_remote_copy(
        src_ref=src, dst_ref=dst, send_sem=send, recv_sem=recv, device_id=device, device_id_type=MESH
    )


def place():
    x, s, tp = lax.axis_index("own"), lax.axis_index("seq"), lax.axis_index("tp")
    return x, s, tp


def spread_kernel(root, w_ref, wo_ref, gain_ref, w_out, wo_out, gain_out, w_mid, wo_mid, gain_mid,
                  send_sem, recv_sem, mid_sem, pass_sem, local_sem):
    x, s, tp = place()
    z, yh = s // 2, s % 2
    far = (root + 2) % 4
    mid = (root + 3) % 4 if ((far ^ 1) - root) % 4 == 1 else (root + 1) % 4

    @pl.when(x == root)
    def _():
        for group in range(4):
            plane = mid if group == far else group
            land = (w_mid, wo_mid, gain_mid) if group == far else (w_out, wo_out, gain_out)
            sems = mid_sem if group == far else recv_sem

            @pl.when(tp == group)
            def _(group=group, plane=plane, land=land, sems=sems):
                for phase in ("start", "wait"):
                    for quarter in range(4):
                        piece = w_ref.at[:, pl.ds(quarter * QUARTER, QUARTER), :]
                        wo_piece = wo_ref.at[pl.ds(quarter * QUARTER, QUARTER), :]
                        near = (plane, s, quarter)
                        wo_dest = (plane, quarter * 2 + yh, z)
                        if plane == root and quarter == group:
                            copies = [
                                pltpu.make_async_copy(piece, land[0], local_sem.at[0]),
                                pltpu.make_async_copy(gain_ref, land[2], local_sem.at[2]),
                            ]
                        else:
                            copies = [
                                remote(piece, land[0], send_sem.at[quarter], sems.at[0], near),
                                remote(gain_ref, land[2], send_sem.at[8 + quarter], sems.at[2], near),
                            ]
                        for copy in copies:
                            if phase == "start":
                                copy.start()
                            elif plane == root and quarter == group:
                                copy.wait()
                            else:
                                copy.wait_send()
                        far_wo = remote(wo_piece, land[1], send_sem.at[4 + quarter], sems.at[1], wo_dest)
                        if plane == root:
                            here = (z == group) & (z == quarter)

                            @pl.when(here)
                            def _(wo_piece=wo_piece, land=land, phase=phase):
                                copy = pltpu.make_async_copy(wo_piece, land[1], local_sem.at[1])
                                copy.start() if phase == "start" else copy.wait()

                            @pl.when(jnp.logical_not(here))
                            def _(far_wo=far_wo, phase=phase):
                                far_wo.start() if phase == "start" else far_wo.wait_send()
                        else:
                            far_wo.start() if phase == "start" else far_wo.wait_send()

    @pl.when(x == mid)
    def _():
        target = (far, s, tp)
        hops = []
        for i, (held, land) in enumerate(((w_mid, w_out), (wo_mid, wo_out), (gain_mid, gain_out))):
            remote(held, held, pass_sem.at[i], mid_sem.at[i], target).wait_recv()
            hop = remote(held, land, pass_sem.at[i], recv_sem.at[i], target)
            hop.start()
            hops.append(hop)
        for hop in hops:
            hop.wait_send()

    def arrive(i, ref):
        remote(ref, ref, send_sem.at[0], recv_sem.at[i], (x, s, tp)).wait_recv()

    at_root = x == root

    @pl.when(jnp.logical_not(at_root & (tp == root)))
    def _():
        arrive(0, w_out)
        arrive(2, gain_out)

    @pl.when(jnp.logical_not(at_root & (tp == root) & (z == root)))
    def _():
        arrive(1, wo_out)


def spread(root, w, wo, gain):
    shapes = [(3, QUARTER, COLS), (QUARTER, COLS), (16, COLS)]
    return pl.pallas_call(
        lambda *refs: spread_kernel(root, *refs),
        out_shape=[jax.ShapeDtypeStruct(shape, jnp.bfloat16) for shape in shapes],
        in_specs=[ANY] * 3,
        out_specs=[ANY] * 3,
        scratch_shapes=[pltpu.VMEM(shape, jnp.bfloat16) for shape in shapes]
        + [
            pltpu.SemaphoreType.DMA((12,)),
            pltpu.SemaphoreType.DMA((3,)),
            pltpu.SemaphoreType.DMA((3,)),
            pltpu.SemaphoreType.DMA((3,)),
            pltpu.SemaphoreType.DMA((3,)),
        ],
        compiler_params=pltpu.CompilerParams(has_side_effects=True, vmem_limit_bytes=16 * 1024 * 1024),
        name=f"spread_{root}",
    )(w, wo, gain)


class Gather:
    def __init__(self, own, slot, dest, half, send_sem, recv_sem, pair_sem):
        self.x, s, tp = place()
        core, yl = tp % 2, tp // 2
        z, y = s // 2, (s % 2) * 2 + yl
        self.core, self.z, self.y = core, z, y
        self.own, self.slot, self.dest, self.half = own, slot, dest, half
        self.send_sem, self.recv_sem, self.pair_sem = send_sem, recv_sem, pair_sem
        self.sent = []

        def device(dz, dy):
            z2, y2 = (z + dz) % 4, (y + dy) % 4
            return (self.x, z2 * 2 + y2 // 2, (y2 % 2) * 2 + core)

        self.first = {d: device((1 - core) * d, core * d) for d in (1, 3)}
        self.second = {d: device(core * d, (1 - core) * d) for d in (1, 3)}
        self.sibling = (self.x, s, tp + 1 - 2 * core)
        self.recv_index = {(1, 0): 0, (3, 0): 1, (2, 0): 2}
        for k in range(4):
            self.recv_index[(k, 1)] = 4 + 4 * k
            self.recv_index[(k, 3)] = 5 + 4 * k
            self.recv_index[(k, 2)] = 6 + 4 * k

    def push(self, src, dst, recv, device):
        copy = remote(src, dst, self.send_sem.at[len(self.sent)], recv, device)
        copy.start()
        self.sent.append(copy)

    def to_sibling(self, k, j, src=None):
        src = self.slot(0, k, j) if src is None else src
        self.push(src, self.dest(1, k, j, k, j), self.pair_sem.at[4 * k + j], self.sibling)

    def along_second(self, k, src=None):
        src = self.slot(0, k, 0) if src is None else src
        for d in (1, 3):
            j = (0 - d) % 4
            self.push(src, self.dest(0, k, 0, k, j), self.recv_sem.at[self.recv_index[(k, j)]], self.second[d])

    def begin(self):
        for d in (1, 3):
            k = (0 - d) % 4
            self.push(self.own, self.dest(0, 0, 0, k, 0), self.recv_sem.at[self.recv_index[(k, 0)]], self.first[d])
        self.along_second(0, self.own)
        self.to_sibling(0, 0, self.own)

    def take(self, ref, sem):
        remote(ref, ref, self.send_sem.at[0], sem, self.sibling).wait_recv()

    def first_near(self, k):
        self.take(self.slot(0, k, 0), self.recv_sem.at[self.recv_index[(k, 0)]])
        h, d = (0, 1) if k == 3 else (1, 3)
        self.push(
            self.half(self.slot(0, k, 0), h), self.half(self.dest(0, k, 0, 2, 0), h),
            self.recv_sem.at[self.recv_index[(2, 0)] + h], self.first[d],
        )
        self.along_second(k)
        self.to_sibling(k, 0)

    def first_far(self):
        for h in range(2):
            self.take(self.half(self.slot(0, 2, 0), h), self.recv_sem.at[self.recv_index[(2, 0)] + h])
        self.along_second(2)
        self.to_sibling(2, 0)

    def second_near(self, k):
        for j in (3, 1):
            self.take(self.slot(0, k, j), self.recv_sem.at[self.recv_index[(k, j)]])
            h, d = (0, 1) if j == 3 else (1, 3)
            self.push(
                self.half(self.slot(0, k, j), h), self.half(self.dest(0, k, j, k, 2), h),
                self.recv_sem.at[self.recv_index[(k, 2)] + h], self.second[d],
            )
            self.to_sibling(k, j)

    def second_far(self, k):
        for h in range(2):
            self.take(self.half(self.slot(0, k, 2), h), self.recv_sem.at[self.recv_index[(k, 2)] + h])
        self.to_sibling(k, 2)

    def from_sibling(self, k, j):
        self.take(self.slot(1, k, j), self.pair_sem.at[4 * k + j])

    def finish(self):
        for copy in self.sent:
            copy.wait_send()


GATHER_SEMS = [
    pltpu.SemaphoreType.DMA((36,)),
    pltpu.SemaphoreType.DMA((20,)),
    pltpu.SemaphoreType.DMA((16,)),
]


def qkv_kernel(xm_ref, w_ref, wo_ref, gain_ref, q_out, kv_out, wo_out,
               wbuf, xbuf, acc, sums, send_sem, recv_sem, pair_sem, x_send, x_recv, x_local,
               wo_send, wo_recv, wo_local, sum_send, sum_recv):
    x, s, tp = place()
    core = tp % 2
    z, yh = s // 2, s % 2
    a0 = z * (1 - core) + ((s % 2) * 2 + tp // 2) * core
    b0 = z * core + ((s % 2) * 2 + tp // 2) * (1 - core)

    def slot(pair, k, j):
        if pair:
            a, b, kind = (b0 + k) % 4, (a0 + j) % 4, 1 - core
        else:
            a, b, kind = (a0 + k) % 4, (b0 + j) % 4, core
        z2 = a * (1 - kind) + b * kind
        y2 = a * kind + b * (1 - kind)
        offset = pl.multiple_of(((y2 % 2) * 2 + kind) * QUARTER, 32)
        return wbuf.at[:, z2 * 2 + y2 // 2, pl.ds(offset, QUARTER), :]

    def dest(pair, k, j, k2, j2):
        return slot(0, k, j)

    def half(ref, h):
        return ref.at[:, pl.ds(h * (QUARTER // 2), QUARTER // 2), :]

    gather = Gather(w_ref, slot, dest, half, send_sem, recv_sem, pair_sem)
    gather.begin()
    own_w = pltpu.make_async_copy(w_ref, slot(0, 0, 0), x_local.at[4])
    own_w.start()

    turn = (x - tp) % 4
    chunk = ROWS // 4
    part = [pl.ds(i * chunk, chunk) for i in range(4)]
    up, down = ((x + 1) % 4, s, tp), ((x + 3) % 4, s, tp)

    def x_send_copy(i, n, device, src):
        return remote(src.at[part[i]], xbuf.at[part[i]], x_send.at[4 * n + i], x_recv.at[i], device)

    @pl.when(turn == 0)
    def _():
        for i in range(4):
            x_send_copy(i, 0, up, xm_ref).start()
            x_send_copy(i, 1, down, xm_ref).start()
            pltpu.make_async_copy(xm_ref.at[part[i]], xbuf.at[part[i]], x_local.at[i]).start()

    relay = turn == 3 - 2 * core
    onward = ((x + 3 + 2 * core) % 4, s, tp)

    def pass_tokens():
        @pl.when(relay)
        def _():
            for i in range(4):
                x_send_copy(i, 0, onward, xbuf).wait_recv()
                x_send_copy(i, 0, onward, xbuf).start()

    def need_tokens():
        @pl.when(turn == 0)
        def _():
            for i in range(4):
                pltpu.make_async_copy(xm_ref.at[part[i]], xbuf.at[part[i]], x_local.at[i]).wait()

        @pl.when((turn != 0) & jnp.logical_not(relay))
        def _():
            for i in range(4):
                x_send_copy(i, 0, up, xbuf).wait_recv()

    acc[...] = jnp.zeros_like(acc)
    gather.first_near(3)
    gather.first_near(1)
    gather.second_near(0)
    gather.first_far()
    gather.second_near(3)
    pass_tokens()
    gather.second_far(0)

    def wo_place(z2, yh2):
        return wo_out.at[pl.ds(pl.multiple_of(z2 * QUARTER, 32), QUARTER), pl.ds(pl.multiple_of(yh2 * COLS, 128), COLS)]

    def wo_copy(i, dz, dy):
        device = (x, ((z + dz) % 4) * 2 + (yh + dy) % 2, tp)
        return remote(wo_ref, wo_place(z, yh), wo_send.at[i], wo_recv.at[i], device)

    offsets = [(1, 0), (3, 0), (0, 1), (1, 1), (3, 1), (2, 0), (2, 1)]

    def dots(first, count):
        def body(i, carry):
            z2 = (z + first + 2 * (i // 2)) % 4
            row = z2 * 2 + i % 2
            tokens = xbuf[:, pl.ds(pl.multiple_of(row * COLS, 128), COLS)]
            for j in range(3):
                acc[j] += jnp.dot(tokens, wbuf[j, row], preferred_element_type=jnp.float32)
            return carry

        lax.fori_loop(0, count, body, 0)

    own_w.wait()
    seen = set()

    def siblings(limit):
        for k in range(4):
            for j in range(4):
                if (k in limit or j in limit) and (k, j) not in seen:
                    seen.add((k, j))
                    gather.from_sibling(k, j)

    gather.second_near(1)
    gather.second_far(3)
    gather.second_near(2)
    siblings((0,))
    need_tokens()
    dots(0, 2)
    gather.second_far(1)
    for i, (dz, dy) in enumerate(offsets):
        wo_copy(i, dz, dy).start()
    own_wo = pltpu.make_async_copy(wo_ref, wo_place(z, yh), wo_local)
    own_wo.start()
    siblings((1, 3))
    dots(1, 4)
    gather.second_far(2)
    siblings((2,))
    dots(2, 2)

    query, key = acc[0], acc[1]
    lane = lax.broadcasted_iota(jnp.int32, (ROWS, 128), 1)
    sums[0] = jnp.where(
        lane == 0, jnp.sum(query * query, axis=1, keepdims=True), jnp.sum(key * key, axis=1, keepdims=True)
    )
    kv_out[:, COLS:] = acc[2].astype(jnp.bfloat16)
    shares = [remote(sums.at[0], sums.at[d], sum_send.at[d], sum_recv.at[d], ((x + d) % 4, s, tp)) for d in (1, 2, 3)]
    for share in shares:
        share.start()
    gains = gain_ref[...].astype(jnp.float32)
    for share in shares:
        share.wait()
    total = (sums[0] + sums[1]) + (sums[2] + sums[3])
    scale = lax.rsqrt(total / HW + EPS)
    q_out[...] = (acc[0] * scale[:, 0:1] * gains[0:1]).astype(jnp.bfloat16)
    kv_out[:, :COLS] = (acc[1] * scale[:, 1:2] * gains[1:2]).astype(jnp.bfloat16)

    @pl.when(turn == 0)
    def _():
        for i in range(4):
            x_send_copy(i, 0, up, xm_ref).wait_send()
            x_send_copy(i, 1, down, xm_ref).wait_send()

    @pl.when(relay)
    def _():
        for i in range(4):
            x_send_copy(i, 0, onward, xbuf).wait_send()

    for i, (dz, dy) in enumerate(offsets):
        copy = wo_copy(i, dz, dy)
        copy.wait_send()
        z2, yh2 = (z + 4 - dz) % 4, (yh + dy) % 2
        remote(wo_ref, wo_place(z2, yh2), wo_send.at[i], wo_recv.at[i], (x, s, tp)).wait_recv()
    own_wo.wait()
    gather.finish()


def qkv_call(xm, w, wo, gain):
    return pl.pallas_call(
        qkv_kernel,
        out_shape=[
            jax.ShapeDtypeStruct((ROWS, COLS), jnp.bfloat16),
            jax.ShapeDtypeStruct((ROWS, 2 * COLS), jnp.bfloat16),
            jax.ShapeDtypeStruct((COLS, 2 * COLS), jnp.bfloat16),
        ],
        in_specs=[ANY, ANY, ANY, VMEM],
        out_specs=[VMEM, VMEM, ANY],
        scratch_shapes=[
            pltpu.VMEM((3, 8, COLS, COLS), jnp.bfloat16),
            pltpu.VMEM((ROWS, D), jnp.bfloat16),
            pltpu.VMEM((3, ROWS, COLS), jnp.float32),
            pltpu.VMEM((4, ROWS, 128), jnp.float32),
            *GATHER_SEMS,
            pltpu.SemaphoreType.DMA((8,)),
            pltpu.SemaphoreType.DMA((4,)),
            pltpu.SemaphoreType.DMA((5,)),
            pltpu.SemaphoreType.DMA((7,)),
            pltpu.SemaphoreType.DMA((7,)),
            pltpu.SemaphoreType.DMA,
            pltpu.SemaphoreType.DMA((4,)),
            pltpu.SemaphoreType.DMA((4,)),
        ],
        compiler_params=pltpu.CompilerParams(has_side_effects=True, vmem_limit_bytes=LIMIT),
        name="qkv",
    )(xm, w, wo, gain)


def attend_kernel(q_ref, kv_ref, wo_ref, inputs_ref, policy_ref, gate_ref, block_out, err_out,
                  kvbuf, wofull, acc, top, low, attn, pair_attn, afull, errs,
                  send_sem, recv_sem, pair_sem, wo_send, wo_recv, local_sem,
                  a_send, a_recv, a_pair_send, a_pair_recv, y_send, y_recv, e_send, e_recv):
    x, s, tp = place()
    core = tp % 2

    def slot(pair, k, j):
        return kvbuf.at[pair, 4 * k + j]

    def dest(pair, k, j, k2, j2):
        return kvbuf.at[pair, 4 * k2 + j2]

    def half(ref, h):
        return ref.at[pl.ds(h * (ROWS // 2), ROWS // 2), :]

    gather = Gather(kv_ref, slot, dest, half, send_sem, recv_sem, pair_sem)
    gather.begin()
    own_kv = pltpu.make_async_copy(kv_ref, slot(0, 0, 0), local_sem.at[0])
    own_kv.start()

    up, down = ((x + 1) % 4, s, tp), ((x + 3) % 4, s, tp)
    rows = [pl.ds(0, COLS // 2), pl.ds(COLS // 2, COLS // 2)]

    def wo_copy(i, src, plane, h, device, n):
        return remote(src, wofull.at[plane, rows[h]], wo_send.at[i], wo_recv.at[n], device)

    own_sends = [
        wo_copy(0, wo_ref.at[rows[0]], x, 0, up, 0),
        wo_copy(1, wo_ref.at[rows[1]], x, 1, down, 1),
        wo_copy(2, wo_ref.at[rows[1]], x, 1, up, 2),
        wo_copy(3, wo_ref.at[rows[0]], x, 0, down, 3),
    ]
    for copy in own_sends:
        copy.start()
    own_wo = pltpu.make_async_copy(wo_ref, wofull.at[x], local_sem.at[1])
    own_wo.start()
    below, above, across = (x + 3) % 4, (x + 1) % 4, (x + 2) % 4
    onward = [
        wo_copy(4, wofull.at[below, rows[0]], below, 0, up, 4),
        wo_copy(5, wofull.at[above, rows[1]], above, 1, down, 5),
    ]

    def pass_wo():
        wo_copy(4, wofull.at[below, rows[0]], below, 0, up, 0).wait_recv()
        onward[0].start()
        wo_copy(5, wofull.at[above, rows[1]], above, 1, down, 1).wait_recv()
        onward[1].start()

    def need_wo():
        own_wo.wait()
        wo_copy(2, wo_ref.at[rows[1]], below, 1, up, 2).wait_recv()
        wo_copy(3, wo_ref.at[rows[0]], above, 0, up, 3).wait_recv()
        wo_copy(4, wo_ref.at[rows[0]], across, 0, up, 4).wait_recv()
        wo_copy(5, wo_ref.at[rows[1]], across, 1, up, 5).wait_recv()

    acc[...] = jnp.zeros_like(acc)
    low[...] = jnp.zeros_like(low)
    top[...] = jnp.full_like(top, -1e30)
    factor = float(HD) ** -0.5 * 1.4426950408889634

    def flash(pair, k):
        def body(h, carry):
            cols = pl.ds(pl.multiple_of(h * HD, HD), HD)
            vcols = pl.ds(pl.multiple_of(COLS + h * HD, HD), HD)
            keys = kvbuf[pair, pl.ds(4 * k, 4), :, cols].reshape(4 * ROWS, HD)
            values = kvbuf[pair, pl.ds(4 * k, 4), :, vcols].reshape(4 * ROWS, HD)
            scores = lax.dot_general(
                q_ref[:, cols], keys, (((1,), (1,)), ((), ())), preferred_element_type=jnp.float32
            )
            old = top[h]
            new = jnp.maximum(old, jnp.max(scores, axis=1, keepdims=True))
            top[h] = new
            decay = jnp.exp2((old - new) * factor)
            probs = jnp.exp2((scores - new[:, 0:1]) * factor)
            part = probs[:, 0:128]
            for i in range(1, 4 * ROWS // 128):
                part = part + probs[:, i * 128 : (i + 1) * 128]
            low[h] = low[h] * decay + part
            acc[h] = acc[h] * decay + jnp.dot(
                probs.astype(jnp.bfloat16), values, preferred_element_type=jnp.float32
            )
            return carry

        lax.fori_loop(0, HEADS_HERE, body, 0)

    def siblings(k):
        for j in range(4):
            gather.from_sibling(k, j)

    gather.first_near(3)
    gather.first_near(1)
    gather.second_near(0)
    gather.first_far()
    gather.second_near(3)
    pass_wo()
    own_kv.wait()
    gather.second_far(0)
    flash(0, 0)
    gather.second_near(1)
    gather.second_far(3)
    siblings(0)
    flash(1, 0)
    flash(0, 3)
    gather.second_near(2)
    gather.second_far(1)
    siblings(3)
    flash(1, 3)
    flash(0, 1)
    gather.second_far(2)
    siblings(1)
    flash(1, 1)
    siblings(2)
    flash(0, 2)
    flash(1, 2)

    for h in range(HEADS_HERE):
        total = jnp.sum(low[h], axis=1, keepdims=True)
        attn[:, h * HD : (h + 1) * HD] = (acc[h] / total).astype(jnp.bfloat16)
    need_wo()

    partner = (tp + 2) % 4
    swap = remote(attn, pair_attn, y_send, y_recv, (x, s, partner))
    swap.start()

    def deliver(i, block, held, phase):
        near = pltpu.make_async_copy(held, afull.at[x], local_sem.at[2 + i])
        away = remote(held, afull.at[x], a_send.at[i], a_recv.at[x], (block, s, tp))

        @pl.when(x == block)
        def _():
            near.start() if phase == 0 else None

        @pl.when(x != block)
        def _():
            away.start() if phase == 0 else away.wait_send()

    deliver(0, tp, attn, 0)
    swap.wait_recv()
    deliver(1, partner, pair_attn, 0)

    mine = x % 2 == core
    sibling = (x, s, tp + 1 - 2 * core)
    proj = None
    for d in (0, 1, 3, 2):
        plane = (x + d) % 4
        pair_copy = remote(afull.at[plane], afull.at[plane], a_pair_send.at[d], a_pair_recv.at[d], sibling)

        @pl.when(mine)
        def _(d=d, plane=plane, pair_copy=pair_copy):
            if d == 0:
                @pl.when(x == tp)
                def _():
                    pltpu.make_async_copy(attn, afull.at[x], local_sem.at[2]).wait()

                @pl.when(x != tp)
                def _():
                    pltpu.make_async_copy(pair_attn, afull.at[x], local_sem.at[3]).wait()
            else:
                remote(attn, afull.at[plane], a_send.at[0], a_recv.at[plane], sibling).wait_recv()
            pair_copy.start()

        @pl.when(jnp.logical_not(mine))
        def _(pair_copy=pair_copy):
            pair_copy.wait_recv()

        term = jnp.dot(afull[plane], wofull[plane], preferred_element_type=jnp.float32)
        proj = term if proj is None else proj + term

    block = (inputs_ref[...].astype(jnp.float32) + gate_ref[0:1] * proj).astype(jnp.bfloat16)
    block_out[...] = block
    differ = block.astype(jnp.float32) - policy_ref[...].astype(jnp.float32)
    errs[0] = jnp.broadcast_to(jnp.sum(differ * differ, axis=1, keepdims=True), (ROWS, 128))
    for i in range(2):
        deliver(i, (tp, partner)[i], (attn, pair_attn)[i], 1)
    swap.wait_send()

    @pl.when(mine)
    def _():
        for d in range(4):
            plane = (x + d) % 4
            remote(afull.at[plane], afull.at[plane], a_pair_send.at[d], a_pair_recv.at[d], sibling).wait_send()

    shares = [remote(errs.at[0], errs.at[d], e_send.at[d], e_recv.at[d], (x, s, (tp + d) % 4)) for d in (1, 2, 3)]
    for share in shares:
        share.start()
    for copy in own_sends + onward:
        copy.wait_send()
    gather.finish()
    for share in shares:
        share.wait()
    err_out[...] = ((errs[0] + errs[1]) + (errs[2] + errs[3])) / D


def attend_call(q, kv, wo, inputs, policy, gate):
    return pl.pallas_call(
        attend_kernel,
        out_shape=[
            jax.ShapeDtypeStruct((ROWS, D // 4), jnp.bfloat16),
            jax.ShapeDtypeStruct((ROWS, 128), jnp.float32),
        ],
        in_specs=[VMEM, ANY, ANY, VMEM, VMEM, VMEM],
        out_specs=[VMEM, VMEM],
        scratch_shapes=[
            pltpu.VMEM((2, 16, ROWS, 2 * COLS), jnp.bfloat16),
            pltpu.VMEM((4, COLS, 2 * COLS), jnp.bfloat16),
            pltpu.VMEM((HEADS_HERE, ROWS, HD), jnp.float32),
            pltpu.VMEM((HEADS_HERE, ROWS, HD), jnp.float32),
            pltpu.VMEM((HEADS_HERE, ROWS, HD), jnp.float32),
            pltpu.VMEM((ROWS, COLS), jnp.bfloat16),
            pltpu.VMEM((ROWS, COLS), jnp.bfloat16),
            pltpu.VMEM((4, ROWS, COLS), jnp.bfloat16),
            pltpu.VMEM((4, ROWS, 128), jnp.float32),
            *GATHER_SEMS,
            pltpu.SemaphoreType.DMA((6,)),
            pltpu.SemaphoreType.DMA((6,)),
            pltpu.SemaphoreType.DMA((4,)),
            pltpu.SemaphoreType.DMA((2,)),
            pltpu.SemaphoreType.DMA((4,)),
            pltpu.SemaphoreType.DMA((4,)),
            pltpu.SemaphoreType.DMA((4,)),
            pltpu.SemaphoreType.DMA,
            pltpu.SemaphoreType.DMA,
            pltpu.SemaphoreType.DMA((4,)),
            pltpu.SemaphoreType.DMA((4,)),
        ],
        compiler_params=pltpu.CompilerParams(has_side_effects=True, vmem_limit_bytes=LIMIT),
        name="attend",
    )(q, kv, wo, inputs, policy, gate)


def local(latents, policy_out, w_qkv, w_out, qk_gains, mod_table, timestep, owner):
    held = w_qkv.shape[0]
    local_block = owner[0] % held
    root_group = owner[0] // held
    mine_qkv = lax.dynamic_index_in_dim(w_qkv.transpose(0, 2, 1, 3), local_block, 0, keepdims=False)
    mine_out = lax.dynamic_index_in_dim(w_out, local_block, 0, keepdims=False)
    mine_gains = lax.dynamic_index_in_dim(qk_gains, local_block, 0, keepdims=False)
    mine_gains = jnp.pad(mine_gains, ((0, 14), (0, 0)))
    w, wo, gain = lax.switch(
        root_group,
        [lambda a, b, c, root=root: tuple(spread(root, a, b, c)) for root in range(4)],
        mine_qkv, mine_out, mine_gains,
    )
    onehot = (jnp.arange(mod_table.shape[0], dtype=jnp.int32) == timestep[0]).astype(jnp.float32)
    modulation = jnp.tensordot(onehot, mod_table, axes=1, precision=lax.Precision.HIGHEST)
    shift, scale, gate = (modulation[0], modulation[1], modulation[2])
    inputs = latents[0].astype(jnp.float32)
    center = jnp.mean(inputs, axis=-1, keepdims=True)
    spread_sq = jnp.mean((inputs - center) ** 2, axis=-1, keepdims=True)
    normed = (inputs - center) * lax.rsqrt(spread_sq + EPS)
    modulated = (normed * (1.0 + scale) + shift).astype(jnp.bfloat16)
    q, kv, wo_rows = qkv_call(modulated, w, wo, gain)
    offset = lax.axis_index("tp") * (D // 4)
    inputs_part = lax.dynamic_slice_in_dim(latents[0], offset, D // 4, 1)
    gate_part = jnp.broadcast_to(lax.dynamic_slice_in_dim(gate, offset, D // 4, 0)[None], (8, D // 4))
    block, squares = attend_call(q, kv, wo_rows, inputs_part, policy_out[0], gate_part)
    return (block[None], squares[:, 0][None])


def solution(mesh):
    placed = (
        P(None, ("own", "seq"), None),
        P(None, ("own", "seq"), "tp"),
        P("own", "seq", None, "tp"),
        P("own", "tp", "seq"),
        P("own", None, "tp"),
        P(),
        P(),
        P(),
    )
    return jax.shard_map(
        local,
        mesh=mesh,
        in_specs=placed,
        out_specs=(P(None, ("own", "seq"), "tp"), P(None, ("own", "seq"))),
        check_vma=False,
    )
```

```python
import jax
import jax.numpy as jnp
from jax import lax
from jax.experimental import pallas as pl
from jax.experimental.pallas import tpu as pltpu
from jax.sharding import PartitionSpec as P

D = 5120
HD = 128
HW = 2560
ROWS = 256
COLS = 640
HEADS_HERE = 5
QUARTER = 160
EPS = 1e-06
MESH = pl.DeviceIdType.MESH
ANY = pl.BlockSpec(memory_space=pl.ANY)
VMEM = pl.BlockSpec(memory_space=pltpu.VMEM)
LIMIT = 62 * 1024 * 1024


def remote(src, dst, send, recv, device):
    return pltpu.make_async_remote_copy(
        src_ref=src, dst_ref=dst, send_sem=send, recv_sem=recv, device_id=device, device_id_type=MESH
    )


def place():
    x, s, tp = lax.axis_index("own"), lax.axis_index("seq"), lax.axis_index("tp")
    return x, s, tp


def greet(devices, extra=None):
    barrier = pltpu.get_barrier_semaphore()
    for device in devices:
        pl.semaphore_signal(barrier, inc=1, device_id=device, device_id_type=MESH)
    if extra is not None:
        extra(barrier)
    pl.semaphore_wait(barrier, len(devices))


def gather_sems(count):
    return [
        pltpu.SemaphoreType.DMA((36 * count,)),
        pltpu.SemaphoreType.DMA((20 * count,)),
        pltpu.SemaphoreType.DMA((16 * count,)),
    ]


def neighbours():
    x, s, tp = place()
    core, z, y = tp % 2, s // 2, (s % 2) * 2 + tp // 2

    def device(dx, dz, dy):
        y2 = (y + dy) % 4
        return ((x + dx) % 4, ((z + dz) % 4) * 2 + y2 // 2, (y2 % 2) * 2 + core)

    return [
        device(0, 1, 0), device(0, 3, 0), device(0, 0, 1), device(0, 0, 3),
        device(1, 0, 0), device(2, 0, 0), device(3, 0, 0), (x, s, tp + 1 - 2 * core),
    ]


class Gather:
    def __init__(self, own, slot, dest, half, send_sem, recv_sem, pair_sem, turn=0):
        self.x, s, tp = place()
        core, yl = tp % 2, tp // 2
        z, y = s // 2, (s % 2) * 2 + yl
        self.core, self.z, self.y = core, z, y
        self.own, self.slot, self.dest, self.half = own, slot, dest, half
        self.send_sem, self.recv_sem, self.pair_sem = send_sem, recv_sem, pair_sem
        self.sent = []
        self.base = (36 * turn, 20 * turn, 16 * turn)

        def device(dz, dy):
            z2, y2 = (z + dz) % 4, (y + dy) % 4
            return (self.x, z2 * 2 + y2 // 2, (y2 % 2) * 2 + core)

        self.first = {d: device((1 - core) * d, core * d) for d in (1, 3)}
        self.second = {d: device(core * d, (1 - core) * d) for d in (1, 3)}
        self.sibling = (self.x, s, tp + 1 - 2 * core)
        self.recv_index = {(1, 0): 0, (3, 0): 1, (2, 0): 2}
        for k in range(4):
            self.recv_index[(k, 1)] = 4 + 4 * k
            self.recv_index[(k, 3)] = 5 + 4 * k
            self.recv_index[(k, 2)] = 6 + 4 * k

    def push(self, src, dst, recv, device):
        copy = remote(src, dst, self.send_sem.at[self.base[0] + len(self.sent)], recv, device)
        copy.start()
        self.sent.append(copy)

    def to_sibling(self, k, j, src=None):
        src = self.slot(0, k, j) if src is None else src
        self.push(src, self.dest(1, k, j, k, j), self.pair_sem.at[self.base[2] + 4 * k + j], self.sibling)

    def along_second(self, k, src=None):
        src = self.slot(0, k, 0) if src is None else src
        for d in (1, 3):
            j = (0 - d) % 4
            self.push(src, self.dest(0, k, 0, k, j), self.recv_sem.at[self.base[1] + self.recv_index[(k, j)]], self.second[d])

    def begin(self):
        for d in (1, 3):
            k = (0 - d) % 4
            self.push(self.own, self.dest(0, 0, 0, k, 0), self.recv_sem.at[self.base[1] + self.recv_index[(k, 0)]], self.first[d])
        self.along_second(0, self.own)
        self.to_sibling(0, 0, self.own)

    def take(self, ref, sem):
        remote(ref, ref, self.send_sem.at[self.base[0]], sem, self.sibling).wait_recv()

    def first_near(self, k):
        self.take(self.slot(0, k, 0), self.recv_sem.at[self.base[1] + self.recv_index[(k, 0)]])
        h, d = (0, 1) if k == 3 else (1, 3)
        self.push(
            self.half(self.slot(0, k, 0), h), self.half(self.dest(0, k, 0, 2, 0), h),
            self.recv_sem.at[self.base[1] + self.recv_index[(2, 0)] + h], self.first[d],
        )
        self.along_second(k)
        self.to_sibling(k, 0)

    def first_far(self):
        for h in range(2):
            self.take(self.half(self.slot(0, 2, 0), h), self.recv_sem.at[self.base[1] + self.recv_index[(2, 0)] + h])
        self.along_second(2)
        self.to_sibling(2, 0)

    def second_near(self, k):
        for j in (3, 1):
            self.take(self.slot(0, k, j), self.recv_sem.at[self.base[1] + self.recv_index[(k, j)]])
            h, d = (0, 1) if j == 3 else (1, 3)
            self.push(
                self.half(self.slot(0, k, j), h), self.half(self.dest(0, k, j, k, 2), h),
                self.recv_sem.at[self.base[1] + self.recv_index[(k, 2)] + h], self.second[d],
            )
            self.to_sibling(k, j)

    def second_far(self, k):
        for h in range(2):
            self.take(self.half(self.slot(0, k, 2), h), self.recv_sem.at[self.base[1] + self.recv_index[(k, 2)] + h])
        self.to_sibling(k, 2)

    def from_sibling(self, k, j):
        self.take(self.slot(1, k, j), self.pair_sem.at[self.base[2] + 4 * k + j])

    def finish(self):
        for copy in self.sent:
            copy.wait_send()


ORDER = (1, 2, 0)


def qkv_kernel(root, w_ref, wo_ref, gain_ref, x_ref, mod_ref, q_out, kv_out, wo_out,
               wbuf, xbuf, xraw, acc, sums, gain, w_mid, wo_mid, gain_mid,
               send_sem, recv_sem, pair_sem, spread_send, spread_recv, mid_recv, mid_send, spread_local,
               x_send, x_recv, x_local, wo_send, wo_recv, sum_send, sum_recv):
    x, s, tp = place()
    core = tp % 2
    z, yh = s // 2, s % 2
    y = yh * 2 + tp // 2
    a0 = z * (1 - core) + y * core
    b0 = z * core + y * (1 - core)
    far = (root + 2) % 4
    mid = (root + 3) % 4 if ((far ^ 1) - root) % 4 == 1 else (root + 1) % 4

    turn_of = (x - tp) % 4

    raw = pltpu.make_async_copy(x_ref, xraw, x_local.at[4])

    @pl.when(turn_of == 0)
    def _():
        raw.start()

    barrier = pltpu.get_barrier_semaphore()
    near = neighbours() + [(x, s + 1 - 2 * yh, tp)]
    for device in near:
        pl.semaphore_signal(barrier, inc=1, device_id=device, device_id_type=MESH)
    for group in range(4):
        @pl.when(jnp.logical_not((x == root) & (tp == group)))
        def _(group=group):
            pl.semaphore_signal(barrier, inc=1, device_id=(root, s, group), device_id_type=MESH)

        @pl.when(jnp.logical_not((x == root) & (tp == group) & (z == tp)))
        def _(group=group):
            pl.semaphore_signal(barrier, inc=1, device_id=(root, tp * 2 + yh, group), device_id_type=MESH)

    greeted = jnp.where(x == root, jnp.where(z == tp, 30, 31), 0)
    pl.semaphore_wait(barrier, len(near) + greeted)

    def quarter_of(ref, j, quarter):
        return ref.at[j, pl.ds(quarter * QUARTER, QUARTER), :]

    def w_place(j, quarter):
        return wbuf.at[j, s, pl.ds(quarter * QUARTER, QUARTER), :]

    def wo_place(z2, yh2):
        return wo_out.at[pl.ds(pl.multiple_of(z2 * QUARTER, 32), QUARTER), pl.ds(pl.multiple_of(yh2 * COLS, 128), COLS)]

    def root_copies(group, act):
        plane = mid if group == far else group
        through = group == far
        sems = mid_recv if through else spread_recv
        for c, j in enumerate(ORDER):
            for quarter in range(4):
                piece = quarter_of(w_ref, j, quarter)
                land = w_mid.at[c] if through else w_place(j, quarter)
                if plane == root and quarter == group:
                    act(pltpu.make_async_copy(piece, land, spread_local.at[c]), True)
                else:
                    act(remote(piece, land, spread_send.at[4 * c + quarter], sems.at[c], (plane, s, quarter)), False)
                if c == 0:
                    land = gain_mid if through else gain
                    if plane == root and quarter == group:
                        act(pltpu.make_async_copy(gain_ref, land, spread_local.at[4]), True)
                    else:
                        act(remote(gain_ref, land, spread_send.at[16 + quarter], sems.at[4], (plane, s, quarter)), False)
        for quarter in range(4):
            piece = wo_ref.at[pl.ds(quarter * QUARTER, QUARTER), :]
            land = wo_mid if through else wo_place(quarter, yh)

            def go(piece=piece, land=land, quarter=quarter):
                act(remote(piece, land, spread_send.at[12 + quarter], sems.at[3], (plane, quarter * 2 + yh, z)), False)

            if plane == root:
                here = (z == group) & (z == quarter)

                @pl.when(here)
                def _(piece=piece, land=land):
                    act(pltpu.make_async_copy(piece, land, spread_local.at[3]), True)

                pl.when(jnp.logical_not(here))(go)
            else:
                go()

    def start(copy, here):
        copy.start()

    def drain(copy, here):
        if not here:
            copy.wait_send()

    @pl.when(x == root)
    def _():
        for group in range(4):
            pl.when(tp == group)(lambda group=group: root_copies(group, start))

    def mid_copy(i):
        held = (w_mid.at[0], w_mid.at[1], w_mid.at[2], wo_mid, gain_mid)[i]
        if i < 3:
            land = wbuf.at[ORDER[i], s, pl.ds(pl.multiple_of(tp * QUARTER, 32), QUARTER), :]
        else:
            land = (wo_place(z, yh), gain)[i - 3]
        return remote(held, held, mid_send.at[i], mid_recv.at[i], (far, s, tp)), remote(
            held, land, mid_send.at[i], spread_recv.at[i], (far, s, tp)
        )

    def relay(i):
        @pl.when(x == mid)
        def _():
            arrived, hop = mid_copy(i)
            arrived.wait_recv()
            hop.start()

    def own_place(i):
        if i < 3:
            return wbuf.at[ORDER[i], s, pl.ds(pl.multiple_of(tp * QUARTER, 32), QUARTER), :]
        return (wo_place(z, yh), gain)[i - 3]

    def arrive(i):
        ref = own_place(i)
        here = (x == root) & (tp == root)
        if i == 3:
            here = here & (z == root)

        @pl.when(here)
        def _():
            pltpu.make_async_copy(ref, ref, spread_local.at[i]).wait()

        @pl.when(jnp.logical_not(here))
        def _():
            remote(ref, ref, spread_send.at[0], spread_recv.at[i], (x, s, tp)).wait_recv()

    def chunk(c):
        j = ORDER[c]

        def slot(pair, k, m):
            if pair:
                a, b, kind = (b0 + k) % 4, (a0 + m) % 4, 1 - core
            else:
                a, b, kind = (a0 + k) % 4, (b0 + m) % 4, core
            z2 = a * (1 - kind) + b * kind
            y2 = a * kind + b * (1 - kind)
            offset = pl.multiple_of(((y2 % 2) * 2 + kind) * QUARTER, 32)
            return wbuf.at[j, z2 * 2 + y2 // 2, pl.ds(offset, QUARTER), :]

        def dest(pair, k, m, k2, m2):
            return slot(0, k, m)

        def half(ref, h):
            return ref.at[pl.ds(h * (QUARTER // 2), QUARTER // 2), :]

        return Gather(slot(0, 0, 0), slot, dest, half, send_sem, recv_sem, pair_sem, c)

    parts = [chunk(c) for c in range(3)]

    rows = ROWS // 4
    part = [pl.ds(i * rows, rows) for i in range(4)]
    up, down = ((x + 1) % 4, s, tp), ((x + 3) % 4, s, tp)
    forward = turn_of == 3 - 2 * core
    onward = ((x + 3 + 2 * core) % 4, s, tp)

    def x_copy(i, n, device):
        return remote(xbuf.at[part[i]], xbuf.at[part[i]], x_send.at[4 * n + i], x_recv.at[i], device)

    def normalize():
        @pl.when(turn_of == 0)
        def _():
            raw.wait()
            shift, scale = mod_ref[0:1], 1.0 + mod_ref[1:2]

            def body(i, carry):
                at = pl.ds(pl.multiple_of(i * 16, 16), 16)
                inputs = xraw[at].astype(jnp.float32)
                center = jnp.mean(inputs, axis=-1, keepdims=True)
                spread = jnp.mean((inputs - center) ** 2, axis=-1, keepdims=True)
                normed = (inputs - center) * lax.rsqrt(spread + EPS)
                xbuf[at] = (normed * scale + shift).astype(jnp.bfloat16)
                return carry

            lax.fori_loop(0, ROWS // 16, body, 0)

    def send_tokens():
        @pl.when(turn_of == 0)
        def _():
            for i in range(4):
                x_copy(i, 0, up).start()
                x_copy(i, 1, down).start()

    def pass_tokens(i):
        @pl.when(forward)
        def _():
            x_copy(i, 0, onward).wait_recv()
            x_copy(i, 0, onward).start()

    def need_tokens():
        @pl.when((turn_of != 0) & jnp.logical_not(forward))
        def _():
            for i in range(4):
                x_copy(i, 0, up).wait_recv()

    def dots(c):
        j = ORDER[c]
        acc[j] = jnp.zeros((ROWS, COLS), jnp.float32)

        def body(row, carry):
            tokens = xbuf[:, pl.ds(pl.multiple_of(row * COLS, 128), COLS)]
            acc[j] += jnp.dot(tokens, wbuf[j, row], preferred_element_type=jnp.float32)
            return carry

        lax.fori_loop(0, 8, body, 0)

    def siblings(c):
        for k in range(4):
            for m in range(4):
                parts[c].from_sibling(k, m)

    def row_sum(j):
        return jnp.broadcast_to(jnp.sum(acc[j] * acc[j], axis=1, keepdims=True), (ROWS, 128))

    def share(n):
        return [
            remote(sums.at[n, 0], sums.at[n, d], sum_send.at[4 * n + d], sum_recv.at[4 * n + d], ((x + d) % 4, s, tp))
            for d in (1, 2, 3)
        ]

    def scale_of(n):
        total = (sums[n, 0] + sums[n, 1]) + (sums[n, 2] + sums[n, 3])
        return lax.rsqrt(total / HW + EPS)[:, 0:1]

    normalize()
    relay(4)
    relay(0)
    arrive(4)
    arrive(0)
    g = parts[0]
    g.begin()
    send_tokens()
    g.first_near(3)
    g.first_near(1)
    g.second_near(0)
    g.first_far()
    relay(1)
    g.second_near(3)
    g.second_near(1)
    g.second_near(2)
    arrive(1)
    before = g
    for c in (1, 2):
        g = parts[c]
        g.begin()
        for k in (0, 3, 1, 2):
            before.second_far(k)
        g.first_near(3)
        g.first_near(1)
        g.second_near(0)
        g.first_far()
        pass_tokens(2 * c - 2)
        if c == 1:
            relay(2)
        g.second_near(3)
        g.second_near(1)
        g.second_near(2)
        pass_tokens(2 * c - 1)
        if c == 1:
            arrive(2)
        before = g

    partner = (x, s + 1 - 2 * yh, tp)
    z_up, z_down = (x, ((z + 1) % 4) * 2 + yh, tp), (x, ((z + 3) % 4) * 2 + yh, tp)
    other = 1 - yh

    def wo_copy(i, z2, yh2, device):
        return remote(wo_place(z2, yh2), wo_place(z2, yh2), wo_send.at[i], wo_recv.at[i], device)

    z_prev, z_next, z_far = (z + 3) % 4, (z + 1) % 4, (z + 2) % 4
    relay(3)
    arrive(3)
    wo_steps = [wo_copy(0, z, yh, partner), wo_copy(1, z, yh, z_up), wo_copy(2, z, yh, z_down)]
    for copy in wo_steps:
        copy.start()

    siblings(0)
    need_tokens()
    dots(0)
    sums[0, 0] = row_sum(1)
    siblings(1)
    key_shares = share(0)
    for copy in key_shares:
        copy.start()

    def wo_more(copy):
        copy.start()
        wo_steps.append(copy)

    wo_copy(0, z, other, partner).wait_recv()
    wo_more(wo_copy(3, z, other, z_up))
    wo_more(wo_copy(4, z, other, z_down))
    dots(1)
    kv_out[:, COLS:] = acc[2].astype(jnp.bfloat16)
    wo_copy(1, z_prev, yh, partner).wait_recv()
    wo_more(wo_copy(5, z_prev, yh, z_up))
    for copy in key_shares:
        copy.wait()
    gains = gain[...].astype(jnp.float32)
    kv_out[:, :COLS] = (acc[1] * scale_of(0) * gains[1:2]).astype(jnp.bfloat16)
    for k in (0, 3, 1, 2):
        before.second_far(k)
    wo_copy(4, z_next, other, partner).wait_recv()
    wo_more(wo_copy(6, z_next, other, z_down))
    siblings(2)
    dots(2)
    sums[1, 0] = row_sum(0)
    wo_copy(2, z_next, yh, partner).wait_recv()
    wo_copy(3, z_prev, other, partner).wait_recv()
    query_shares = share(1)
    for copy in query_shares:
        copy.start()
    for gather in parts:
        gather.finish()

    @pl.when(x == root)
    def _():
        for group in range(4):
            pl.when(tp == group)(lambda group=group: root_copies(group, drain))

    @pl.when(x == mid)
    def _():
        for i in range(5):
            mid_copy(i)[1].wait_send()

    @pl.when(turn_of == 0)
    def _():
        for i in range(4):
            x_copy(i, 0, up).wait_send()
            x_copy(i, 1, down).wait_send()

    @pl.when(forward)
    def _():
        for i in range(4):
            x_copy(i, 0, onward).wait_send()

    for copy in query_shares:
        copy.wait()
    q_out[...] = (acc[0] * scale_of(1) * gains[0:1]).astype(jnp.bfloat16)
    wo_copy(5, z_far, yh, partner).wait_recv()
    wo_copy(6, z_far, other, partner).wait_recv()
    for copy in wo_steps:
        copy.wait_send()


def qkv_call(root, w, wo, gain, x, mod):
    return pl.pallas_call(
        lambda *refs: qkv_kernel(root, *refs),
        out_shape=[
            jax.ShapeDtypeStruct((ROWS, COLS), jnp.bfloat16),
            jax.ShapeDtypeStruct((ROWS, 2 * COLS), jnp.bfloat16),
            jax.ShapeDtypeStruct((COLS, 2 * COLS), jnp.bfloat16),
        ],
        in_specs=[ANY, ANY, ANY, ANY, VMEM],
        out_specs=[VMEM, VMEM, ANY],
        scratch_shapes=[
            pltpu.VMEM((3, 8, COLS, COLS), jnp.bfloat16),
            pltpu.VMEM((ROWS, D), jnp.bfloat16),
            pltpu.VMEM((ROWS, D), jnp.bfloat16),
            pltpu.VMEM((3, ROWS, COLS), jnp.float32),
            pltpu.VMEM((2, 4, ROWS, 128), jnp.float32),
            pltpu.VMEM((16, COLS), jnp.bfloat16),
            pltpu.VMEM((3, QUARTER, COLS), jnp.bfloat16),
            pltpu.VMEM((QUARTER, COLS), jnp.bfloat16),
            pltpu.VMEM((16, COLS), jnp.bfloat16),
            *gather_sems(3),
            pltpu.SemaphoreType.DMA((20,)),
            pltpu.SemaphoreType.DMA((5,)),
            pltpu.SemaphoreType.DMA((5,)),
            pltpu.SemaphoreType.DMA((5,)),
            pltpu.SemaphoreType.DMA((5,)),
            pltpu.SemaphoreType.DMA((8,)),
            pltpu.SemaphoreType.DMA((4,)),
            pltpu.SemaphoreType.DMA((5,)),
            pltpu.SemaphoreType.DMA((7,)),
            pltpu.SemaphoreType.DMA((7,)),
            pltpu.SemaphoreType.DMA((8,)),
            pltpu.SemaphoreType.DMA((8,)),
        ],
        compiler_params=pltpu.CompilerParams(has_side_effects=True, vmem_limit_bytes=LIMIT, collective_id=1 + root),
        name=f"qkv_{root}",
    )(w, wo, gain, x, mod)


def attend_kernel(q_ref, kv_ref, wo_ref, x_ref, policy_ref, mod_ref, block_out, err_out,
                  inputs_ref, gate_ref, kvbuf, wofull, acc, top, low, attn, pair_attn, afull, proj, errs,
                  send_sem, recv_sem, pair_sem, wo_send, wo_recv, local_sem,
                  a_send, a_recv, a_pair_send, a_pair_recv, y_send, y_recv, e_send, e_recv):
    x, s, tp = place()
    core = tp % 2
    share_cols = pl.ds(pl.multiple_of(tp * (D // 4), 128), D // 4)
    own_inputs = pltpu.make_async_copy(x_ref.at[:, share_cols], inputs_ref, local_sem.at[6])
    own_gate = pltpu.make_async_copy(mod_ref.at[:, share_cols], gate_ref, local_sem.at[7])
    own_inputs.start()
    own_gate.start()
    greet(neighbours() + [(x, s, 3 - tp)])

    def slot(pair, k, j):
        return kvbuf.at[pair, 4 * k + j]

    def dest(pair, k, j, k2, j2):
        return kvbuf.at[pair, 4 * k2 + j2]

    def half(ref, h):
        return ref.at[pl.ds(h * (ROWS // 2), ROWS // 2), :]

    gather = Gather(kv_ref, slot, dest, half, send_sem, recv_sem, pair_sem)
    gather.begin()
    own_kv = pltpu.make_async_copy(kv_ref, slot(0, 0, 0), local_sem.at[0])
    own_kv.start()

    up, down = ((x + 1) % 4, s, tp), ((x + 3) % 4, s, tp)
    rows = [pl.ds(0, COLS // 2), pl.ds(COLS // 2, COLS // 2)]

    def wo_copy(i, src, plane, h, device, n):
        return remote(src, wofull.at[plane, rows[h]], wo_send.at[i], wo_recv.at[n], device)

    own_sends = [
        wo_copy(0, wo_ref.at[rows[0]], x, 0, up, 0),
        wo_copy(1, wo_ref.at[rows[1]], x, 1, down, 1),
        wo_copy(2, wo_ref.at[rows[1]], x, 1, up, 2),
        wo_copy(3, wo_ref.at[rows[0]], x, 0, down, 3),
    ]
    for copy in own_sends:
        copy.start()
    own_wo = pltpu.make_async_copy(wo_ref, wofull.at[x], local_sem.at[1])
    own_wo.start()
    below, above, across = (x + 3) % 4, (x + 1) % 4, (x + 2) % 4
    onward = [
        wo_copy(4, wofull.at[below, rows[0]], below, 0, up, 4),
        wo_copy(5, wofull.at[above, rows[1]], above, 1, down, 5),
    ]

    def pass_wo():
        wo_copy(4, wofull.at[below, rows[0]], below, 0, up, 0).wait_recv()
        onward[0].start()
        wo_copy(5, wofull.at[above, rows[1]], above, 1, down, 1).wait_recv()
        onward[1].start()

    def need_wo():
        own_wo.wait()
        wo_copy(2, wo_ref.at[rows[1]], below, 1, up, 2).wait_recv()
        wo_copy(3, wo_ref.at[rows[0]], above, 0, up, 3).wait_recv()
        wo_copy(4, wo_ref.at[rows[0]], across, 0, up, 4).wait_recv()
        wo_copy(5, wo_ref.at[rows[1]], across, 1, up, 5).wait_recv()

    acc[...] = jnp.zeros_like(acc)
    low[...] = jnp.zeros_like(low)
    top[...] = jnp.full_like(top, -1e30)
    factor = float(HD) ** -0.5 * 1.4426950408889634

    def step(h, pair, k):
        cols = pl.ds(pl.multiple_of(h * HD, HD), HD)
        vcols = pl.ds(pl.multiple_of(COLS + h * HD, HD), HD)
        keys = kvbuf[pair, pl.ds(4 * k, 4), :, cols].reshape(4 * ROWS, HD)
        values = kvbuf[pair, pl.ds(4 * k, 4), :, vcols].reshape(4 * ROWS, HD)
        scores = lax.dot_general(
            q_ref[:, cols], keys, (((1,), (1,)), ((), ())), preferred_element_type=jnp.float32
        )
        old = top[h]
        new = jnp.maximum(old, jnp.max(scores, axis=1, keepdims=True))
        top[h] = new
        decay = jnp.exp2((old - new) * factor)
        probs = jnp.exp2((scores - new[:, 0:1]) * factor)
        part = probs[:, 0:128]
        for i in range(1, 4 * ROWS // 128):
            part = part + probs[:, i * 128 : (i + 1) * 128]
        low[h] = low[h] * decay + part
        acc[h] = acc[h] * decay + jnp.dot(probs.astype(jnp.bfloat16), values, preferred_element_type=jnp.float32)

    def flash(pair, k):
        def body(h, carry):
            step(h, pair, k)
            return carry

        lax.fori_loop(0, HEADS_HERE, body, 0)

    def siblings(k):
        for j in range(4):
            gather.from_sibling(k, j)

    gather.first_near(3)
    gather.first_near(1)
    gather.second_near(0)
    gather.first_far()
    gather.second_near(3)
    pass_wo()
    own_kv.wait()
    gather.second_far(0)
    flash(0, 0)
    gather.second_near(1)
    gather.second_far(3)
    siblings(0)
    flash(1, 0)
    flash(0, 3)
    gather.second_near(2)
    gather.second_far(1)
    siblings(3)
    flash(1, 3)
    flash(0, 1)
    gather.second_far(2)
    siblings(1)
    flash(1, 1)
    siblings(2)

    partner = (tp + 2) % 4
    sibling = (x, s, tp + 1 - 2 * core)
    mine = x % 2 == core
    spans = [pl.ds(0, 3 * HD), pl.ds(3 * HD, 2 * HD)]

    def swap(g):
        return remote(attn.at[:, spans[g]], pair_attn.at[:, spans[g]], y_send.at[g], y_recv.at[g], (x, s, partner))

    def near(i, g):
        held = (attn, pair_attn)[i]
        return pltpu.make_async_copy(held.at[:, spans[g]], afull.at[x, :, spans[g]], local_sem.at[2 + 2 * i + g])

    def away(i, g, plane):
        held = (attn, pair_attn)[i]
        return remote(
            held.at[:, spans[g]], afull.at[plane, :, spans[g]], a_send.at[2 * i + g], a_recv.at[2 * plane + g],
            ((tp, partner)[i], s, tp),
        )

    def deliver(i, g):
        block = (tp, partner)[i]

        @pl.when(x == block)
        def _():
            near(i, g).start()

        @pl.when(x != block)
        def _():
            away(i, g, x).start()

    def pair_copy(g, d):
        ref = afull.at[(x + d) % 4, :, spans[g]]
        return remote(ref, ref, a_pair_send.at[4 * g + d], a_pair_recv.at[4 * g + d], sibling)

    def collect(g, d):
        @pl.when(mine)
        def _():
            if d == 0:
                @pl.when(x == tp)
                def _():
                    near(0, g).wait()

                @pl.when(x != tp)
                def _():
                    near(1, g).wait()
            else:
                away(0, g, (x + d) % 4).wait_recv()
            pair_copy(g, d).start()

        @pl.when(jnp.logical_not(mine))
        def _():
            pair_copy(g, d).wait_recv()

    def last(h, carry):
        step(h, 0, 2)
        step(h, 1, 2)
        total = jnp.sum(low[h], axis=1, keepdims=True)
        attn[:, pl.ds(pl.multiple_of(h * HD, HD), HD)] = (acc[h] / total).astype(jnp.bfloat16)

        @pl.when(h == 3)
        def _():
            swap(0).start()
            deliver(0, 0)

        return carry

    lax.fori_loop(0, HEADS_HERE, last, 0)
    need_wo()
    swap(1).start()
    deliver(0, 1)
    swap(0).wait_recv()
    deliver(1, 0)

    def project(g, d):
        plane = (x + d) % 4
        first, count = ((0, 3 * HD), (3 * HD, 2 * HD))[g]
        return jnp.dot(
            afull[plane, :, first : first + count], wofull[plane, first : first + count, :],
            preferred_element_type=jnp.float32,
        )

    swap(1).wait_recv()
    deliver(1, 1)
    for d in (0, 1, 3, 2):
        collect(0, d)
        if d == 0:
            proj[...] = project(0, d)
        else:
            proj[...] += project(0, d)
    for d in (0, 1, 3, 2):
        collect(1, d)
        proj[...] += project(1, d)

    own_inputs.wait()
    own_gate.wait()
    block = (inputs_ref[...].astype(jnp.float32) + gate_ref[2:3] * proj[...]).astype(jnp.bfloat16)
    block_out[...] = block
    differ = block.astype(jnp.float32) - policy_ref[...].astype(jnp.float32)
    errs[0] = jnp.broadcast_to(jnp.sum(differ * differ, axis=1, keepdims=True), (ROWS, 128))
    for i in range(2):
        for g in range(2):
            @pl.when(x != (tp, partner)[i])
            def _(i=i, g=g):
                away(i, g, x).wait_send()
    for g in range(2):
        swap(g).wait_send()

    @pl.when(mine)
    def _():
        for g in range(2):
            for d in range(4):
                pair_copy(g, d).wait_send()

    shares = [remote(errs.at[0], errs.at[d], e_send.at[d], e_recv.at[d], (x, s, (tp + d) % 4)) for d in (1, 2, 3)]
    for share in shares:
        share.start()
    for copy in own_sends + onward:
        copy.wait_send()
    gather.finish()
    for share in shares:
        share.wait()
    err_out[...] = ((errs[0] + errs[1]) + (errs[2] + errs[3])) / D


def attend_call(q, kv, wo, x, policy, mod):
    return pl.pallas_call(
        attend_kernel,
        out_shape=[
            jax.ShapeDtypeStruct((ROWS, D // 4), jnp.bfloat16),
            jax.ShapeDtypeStruct((ROWS, 128), jnp.float32),
        ],
        in_specs=[VMEM, ANY, ANY, ANY, VMEM, ANY],
        out_specs=[VMEM, VMEM],
        scratch_shapes=[
            pltpu.VMEM((ROWS, D // 4), jnp.bfloat16),
            pltpu.VMEM((8, D // 4), jnp.float32),
            pltpu.VMEM((2, 16, ROWS, 2 * COLS), jnp.bfloat16),
            pltpu.VMEM((4, COLS, 2 * COLS), jnp.bfloat16),
            pltpu.VMEM((HEADS_HERE, ROWS, HD), jnp.float32),
            pltpu.VMEM((HEADS_HERE, ROWS, HD), jnp.float32),
            pltpu.VMEM((HEADS_HERE, ROWS, HD), jnp.float32),
            pltpu.VMEM((ROWS, COLS), jnp.bfloat16),
            pltpu.VMEM((ROWS, COLS), jnp.bfloat16),
            pltpu.VMEM((4, ROWS, COLS), jnp.bfloat16),
            pltpu.VMEM((ROWS, D // 4), jnp.float32),
            pltpu.VMEM((4, ROWS, 128), jnp.float32),
            *gather_sems(1),
            pltpu.SemaphoreType.DMA((6,)),
            pltpu.SemaphoreType.DMA((6,)),
            pltpu.SemaphoreType.DMA((8,)),
            pltpu.SemaphoreType.DMA((4,)),
            pltpu.SemaphoreType.DMA((8,)),
            pltpu.SemaphoreType.DMA((8,)),
            pltpu.SemaphoreType.DMA((8,)),
            pltpu.SemaphoreType.DMA((2,)),
            pltpu.SemaphoreType.DMA((2,)),
            pltpu.SemaphoreType.DMA((4,)),
            pltpu.SemaphoreType.DMA((4,)),
        ],
        compiler_params=pltpu.CompilerParams(has_side_effects=True, vmem_limit_bytes=LIMIT, collective_id=5),
        name="attend",
    )(q, kv, wo, x, policy, mod)


def local(latents, policy_out, w_qkv, w_out, qk_gains, mod_table, timestep, owner):
    held = w_qkv.shape[0]
    local_block = owner[0] % held
    root_group = owner[0] // held
    mine_qkv = lax.dynamic_index_in_dim(w_qkv.transpose(0, 2, 1, 3), local_block, 0, keepdims=False)
    mine_out = lax.dynamic_index_in_dim(w_out, local_block, 0, keepdims=False)
    mine_gains = lax.dynamic_index_in_dim(qk_gains, local_block, 0, keepdims=False)
    mine_gains = jnp.pad(mine_gains, ((0, 14), (0, 0)))
    onehot = (jnp.arange(mod_table.shape[0], dtype=jnp.int32) == timestep[0]).astype(jnp.float32)
    modulation = jnp.tensordot(onehot, mod_table, axes=1, precision=lax.Precision.HIGHEST)
    mod = jnp.pad(modulation, ((0, 5), (0, 0)))
    q, kv, wo_rows = lax.switch(
        root_group,
        [lambda *a, root=root: tuple(qkv_call(root, *a)) for root in range(4)],
        mine_qkv, mine_out, mine_gains, latents[0], mod,
    )
    block, squares = attend_call(q, kv, wo_rows, latents[0], policy_out[0], mod)
    return (block[None], squares[:, 0][None])


def solution(mesh):
    placed = (
        P(None, ("own", "seq"), None),
        P(None, ("own", "seq"), "tp"),
        P("own", "seq", None, "tp"),
        P("own", "tp", "seq"),
        P("own", None, "tp"),
        P(),
        P(),
        P(),
    )
    return jax.shard_map(
        local,
        mesh=mesh,
        in_specs=placed,
        out_specs=(P(None, ("own", "seq"), "tp"), P(None, ("own", "seq"))),
        check_vma=False,
    )
```

```python
import jax
import jax.numpy as jnp
from jax import lax
from jax.experimental import pallas as pl
from jax.experimental.pallas import tpu as pltpu
from jax.sharding import PartitionSpec as P

D = 5120
HD = 128
HW = 2560
ROWS = 256
COLS = 640
HEADS_HERE = 5
QUARTER = 160
EPS = 1e-06
MESH = pl.DeviceIdType.MESH
ANY = pl.BlockSpec(memory_space=pl.ANY)
VMEM = pl.BlockSpec(memory_space=pltpu.VMEM)
LIMIT = 62 * 1024 * 1024


def remote(src, dst, send, recv, device):
    return pltpu.make_async_remote_copy(
        src_ref=src, dst_ref=dst, send_sem=send, recv_sem=recv, device_id=device, device_id_type=MESH
    )


def place():
    x, s, tp = lax.axis_index("own"), lax.axis_index("seq"), lax.axis_index("tp")
    return x, s, tp


def greet(devices, extra=None):
    barrier = pltpu.get_barrier_semaphore()
    for device in devices:
        pl.semaphore_signal(barrier, inc=1, device_id=device, device_id_type=MESH)
    if extra is not None:
        extra(barrier)
    pl.semaphore_wait(barrier, len(devices))


def to_row(column):
    return jnp.transpose(jnp.broadcast_to(column, (ROWS, 128)))[0:8]


def to_column(row):
    return jnp.transpose(jnp.broadcast_to(row[0:1], (128, ROWS)))[:, 0:1]


def gather_sems(count):
    return [
        pltpu.SemaphoreType.DMA((36 * count,)),
        pltpu.SemaphoreType.DMA((20 * count,)),
        pltpu.SemaphoreType.DMA((16 * count,)),
    ]


def neighbours():
    x, s, tp = place()
    core, z, y = tp % 2, s // 2, (s % 2) * 2 + tp // 2

    def device(dx, dz, dy):
        y2 = (y + dy) % 4
        return ((x + dx) % 4, ((z + dz) % 4) * 2 + y2 // 2, (y2 % 2) * 2 + core)

    return [
        device(0, 1, 0), device(0, 3, 0), device(0, 0, 1), device(0, 0, 3),
        device(1, 0, 0), device(2, 0, 0), device(3, 0, 0), (x, s, tp + 1 - 2 * core),
    ]


class Gather:
    def __init__(self, own, slot, dest, half, send_sem, recv_sem, pair_sem, turn=0):
        self.x, s, tp = place()
        core, yl = tp % 2, tp // 2
        z, y = s // 2, (s % 2) * 2 + yl
        self.core, self.z, self.y = core, z, y
        self.own, self.slot, self.dest, self.half = own, slot, dest, half
        self.send_sem, self.recv_sem, self.pair_sem = send_sem, recv_sem, pair_sem
        self.sent = []
        self.base = (36 * turn, 20 * turn, 16 * turn)

        def device(dz, dy):
            z2, y2 = (z + dz) % 4, (y + dy) % 4
            return (self.x, z2 * 2 + y2 // 2, (y2 % 2) * 2 + core)

        self.first = {d: device((1 - core) * d, core * d) for d in (1, 3)}
        self.second = {d: device(core * d, (1 - core) * d) for d in (1, 3)}
        self.sibling = (self.x, s, tp + 1 - 2 * core)
        self.recv_index = {(1, 0): 0, (3, 0): 1, (2, 0): 2}
        for k in range(4):
            self.recv_index[(k, 1)] = 4 + 4 * k
            self.recv_index[(k, 3)] = 5 + 4 * k
            self.recv_index[(k, 2)] = 6 + 4 * k

    def push(self, src, dst, recv, device):
        copy = remote(src, dst, self.send_sem.at[self.base[0] + len(self.sent)], recv, device)
        copy.start()
        self.sent.append(copy)

    def to_sibling(self, k, j, src=None):
        src = self.slot(0, k, j) if src is None else src
        self.push(src, self.dest(1, k, j, k, j), self.pair_sem.at[self.base[2] + 4 * k + j], self.sibling)

    def along_second(self, k, src=None):
        src = self.slot(0, k, 0) if src is None else src
        for d in (1, 3):
            j = (0 - d) % 4
            self.push(src, self.dest(0, k, 0, k, j), self.recv_sem.at[self.base[1] + self.recv_index[(k, j)]], self.second[d])

    def begin(self):
        for d in (1, 3):
            k = (0 - d) % 4
            self.push(self.own, self.dest(0, 0, 0, k, 0), self.recv_sem.at[self.base[1] + self.recv_index[(k, 0)]], self.first[d])
        self.along_second(0, self.own)
        self.to_sibling(0, 0, self.own)

    def take(self, ref, sem):
        remote(ref, ref, self.send_sem.at[self.base[0]], sem, self.sibling).wait_recv()

    def first_near(self, k):
        self.take(self.slot(0, k, 0), self.recv_sem.at[self.base[1] + self.recv_index[(k, 0)]])
        h, d = (0, 1) if k == 3 else (1, 3)
        self.push(
            self.half(self.slot(0, k, 0), h), self.half(self.dest(0, k, 0, 2, 0), h),
            self.recv_sem.at[self.base[1] + self.recv_index[(2, 0)] + h], self.first[d],
        )
        self.along_second(k)
        self.to_sibling(k, 0)

    def first_far(self):
        for h in range(2):
            self.take(self.half(self.slot(0, 2, 0), h), self.recv_sem.at[self.base[1] + self.recv_index[(2, 0)] + h])
        self.along_second(2)
        self.to_sibling(2, 0)

    def second_near(self, k):
        for j in (3, 1):
            self.take(self.slot(0, k, j), self.recv_sem.at[self.base[1] + self.recv_index[(k, j)]])
            h, d = (0, 1) if j == 3 else (1, 3)
            self.push(
                self.half(self.slot(0, k, j), h), self.half(self.dest(0, k, j, k, 2), h),
                self.recv_sem.at[self.base[1] + self.recv_index[(k, 2)] + h], self.second[d],
            )
            self.to_sibling(k, j)

    def second_far(self, k):
        for h in range(2):
            self.take(self.half(self.slot(0, k, 2), h), self.recv_sem.at[self.base[1] + self.recv_index[(k, 2)] + h])
        self.to_sibling(k, 2)

    def from_sibling(self, k, j):
        self.take(self.slot(1, k, j), self.pair_sem.at[self.base[2] + 4 * k + j])

    def finish(self):
        for copy in self.sent:
            copy.wait_send()


ORDER = (1, 2, 0)


def qkv_kernel(root, w_ref, wo_ref, gain_ref, x_ref, mod_ref, q_out, kv_out, wo_out,
               wbuf, xbuf, xraw, acc, sums, gain, w_mid, wo_mid, gain_mid,
               send_sem, recv_sem, pair_sem, spread_send, spread_recv, mid_recv, mid_send, spread_local,
               x_send, x_recv, x_local, wo_send, wo_recv, sum_send, sum_recv):
    x, s, tp = place()
    core = tp % 2
    z, yh = s // 2, s % 2
    y = yh * 2 + tp // 2
    a0 = z * (1 - core) + y * core
    b0 = z * core + y * (1 - core)
    far = (root + 2) % 4
    mid = (root + 3) % 4 if ((far ^ 1) - root) % 4 == 1 else (root + 1) % 4

    turn_of = (x - tp) % 4

    raw = pltpu.make_async_copy(x_ref, xraw, x_local.at[4])

    @pl.when(turn_of == 0)
    def _():
        raw.start()

    barrier = pltpu.get_barrier_semaphore()
    near = neighbours() + [(x, s + 1 - 2 * yh, tp)]
    for device in near:
        pl.semaphore_signal(barrier, inc=1, device_id=device, device_id_type=MESH)
    for group in range(4):
        @pl.when(jnp.logical_not((x == root) & (tp == group)))
        def _(group=group):
            pl.semaphore_signal(barrier, inc=1, device_id=(root, s, group), device_id_type=MESH)

        @pl.when(jnp.logical_not((x == root) & (tp == group) & (z == tp)))
        def _(group=group):
            pl.semaphore_signal(barrier, inc=1, device_id=(root, tp * 2 + yh, group), device_id_type=MESH)

    greeted = jnp.where(x == root, jnp.where(z == tp, 30, 31), 0)
    pl.semaphore_wait(barrier, len(near) + greeted)

    def quarter_of(ref, j, quarter):
        return ref.at[j, pl.ds(quarter * QUARTER, QUARTER), :]

    def w_place(j, quarter):
        return wbuf.at[j, s, pl.ds(quarter * QUARTER, QUARTER), :]

    def wo_place(z2, yh2):
        return wo_out.at[pl.ds(pl.multiple_of(z2 * QUARTER, 32), QUARTER), pl.ds(pl.multiple_of(yh2 * COLS, 128), COLS)]

    def root_copies(group, act):
        plane = mid if group == far else group
        through = group == far
        sems = mid_recv if through else spread_recv
        for c, j in enumerate(ORDER):
            for quarter in range(4):
                piece = quarter_of(w_ref, j, quarter)
                land = w_mid.at[c] if through else w_place(j, quarter)
                if plane == root and quarter == group:
                    act(pltpu.make_async_copy(piece, land, spread_local.at[c]), True)
                else:
                    act(remote(piece, land, spread_send.at[4 * c + quarter], sems.at[c], (plane, s, quarter)), False)
                if c == 0:
                    land = gain_mid if through else gain
                    if plane == root and quarter == group:
                        act(pltpu.make_async_copy(gain_ref, land, spread_local.at[4]), True)
                    else:
                        act(remote(gain_ref, land, spread_send.at[16 + quarter], sems.at[4], (plane, s, quarter)), False)
        for quarter in range(4):
            piece = wo_ref.at[pl.ds(quarter * QUARTER, QUARTER), :]
            land = wo_mid if through else wo_place(quarter, yh)

            def go(piece=piece, land=land, quarter=quarter):
                act(remote(piece, land, spread_send.at[12 + quarter], sems.at[3], (plane, quarter * 2 + yh, z)), False)

            if plane == root:
                here = (z == group) & (z == quarter)

                @pl.when(here)
                def _(piece=piece, land=land):
                    act(pltpu.make_async_copy(piece, land, spread_local.at[3]), True)

                pl.when(jnp.logical_not(here))(go)
            else:
                go()

    def start(copy, here):
        copy.start()

    def drain(copy, here):
        if not here:
            copy.wait_send()

    @pl.when(x == root)
    def _():
        for group in range(4):
            pl.when(tp == group)(lambda group=group: root_copies(group, start))

    def mid_copy(i):
        held = (w_mid.at[0], w_mid.at[1], w_mid.at[2], wo_mid, gain_mid)[i]
        if i < 3:
            land = wbuf.at[ORDER[i], s, pl.ds(pl.multiple_of(tp * QUARTER, 32), QUARTER), :]
        else:
            land = (wo_place(z, yh), gain)[i - 3]
        return remote(held, held, mid_send.at[i], mid_recv.at[i], (far, s, tp)), remote(
            held, land, mid_send.at[i], spread_recv.at[i], (far, s, tp)
        )

    def relay(i):
        @pl.when(x == mid)
        def _():
            arrived, hop = mid_copy(i)
            arrived.wait_recv()
            hop.start()

    def own_place(i):
        if i < 3:
            return wbuf.at[ORDER[i], s, pl.ds(pl.multiple_of(tp * QUARTER, 32), QUARTER), :]
        return (wo_place(z, yh), gain)[i - 3]

    def arrive(i):
        ref = own_place(i)
        here = (x == root) & (tp == root)
        if i == 3:
            here = here & (z == root)

        @pl.when(here)
        def _():
            pltpu.make_async_copy(ref, ref, spread_local.at[i]).wait()

        @pl.when(jnp.logical_not(here))
        def _():
            remote(ref, ref, spread_send.at[0], spread_recv.at[i], (x, s, tp)).wait_recv()

    def chunk(c):
        j = ORDER[c]

        def slot(pair, k, m):
            if pair:
                a, b, kind = (b0 + k) % 4, (a0 + m) % 4, 1 - core
            else:
                a, b, kind = (a0 + k) % 4, (b0 + m) % 4, core
            z2 = a * (1 - kind) + b * kind
            y2 = a * kind + b * (1 - kind)
            offset = pl.multiple_of(((y2 % 2) * 2 + kind) * QUARTER, 32)
            return wbuf.at[j, z2 * 2 + y2 // 2, pl.ds(offset, QUARTER), :]

        def dest(pair, k, m, k2, m2):
            return slot(0, k, m)

        def half(ref, h):
            return ref.at[pl.ds(h * (QUARTER // 2), QUARTER // 2), :]

        return Gather(slot(0, 0, 0), slot, dest, half, send_sem, recv_sem, pair_sem, c)

    parts = [chunk(c) for c in range(3)]

    rows = ROWS // 4
    part = [pl.ds(i * rows, rows) for i in range(4)]
    up, down = ((x + 1) % 4, s, tp), ((x + 3) % 4, s, tp)
    forward = turn_of == 3 - 2 * core
    onward = ((x + 3 + 2 * core) % 4, s, tp)

    def x_copy(i, n, device):
        return remote(xbuf.at[part[i]], xbuf.at[part[i]], x_send.at[4 * n + i], x_recv.at[i], device)

    def normalize():
        @pl.when(turn_of == 0)
        def _():
            raw.wait()
            shift, scale = mod_ref[0:1], 1.0 + mod_ref[1:2]

            def body(i, carry):
                at = pl.ds(pl.multiple_of(i * 16, 16), 16)
                inputs = xraw[at].astype(jnp.float32)
                center = jnp.mean(inputs, axis=-1, keepdims=True)
                spread = jnp.mean((inputs - center) ** 2, axis=-1, keepdims=True)
                normed = (inputs - center) * lax.rsqrt(spread + EPS)
                xbuf[at] = (normed * scale + shift).astype(jnp.bfloat16)
                return carry

            lax.fori_loop(0, ROWS // 16, body, 0)

    def send_tokens():
        @pl.when(turn_of == 0)
        def _():
            for i in range(4):
                x_copy(i, 0, up).start()
                x_copy(i, 1, down).start()

    def pass_tokens(i):
        @pl.when(forward)
        def _():
            x_copy(i, 0, onward).wait_recv()
            x_copy(i, 0, onward).start()

    def need_tokens():
        @pl.when((turn_of != 0) & jnp.logical_not(forward))
        def _():
            for i in range(4):
                x_copy(i, 0, up).wait_recv()

    def dots(c):
        j = ORDER[c]
        acc[j] = jnp.zeros((ROWS, COLS), jnp.float32)

        def body(row, carry):
            tokens = xbuf[:, pl.ds(pl.multiple_of(row * COLS, 128), COLS)]
            acc[j] += jnp.dot(tokens, wbuf[j, row], preferred_element_type=jnp.float32)
            return carry

        lax.fori_loop(0, 8, body, 0)

    def siblings(c):
        for k in range(4):
            for m in range(4):
                parts[c].from_sibling(k, m)

    def row_sum(j):
        return to_row(jnp.sum(acc[j] * acc[j], axis=1, keepdims=True))

    def share(n):
        return [
            remote(sums.at[n, 0], sums.at[n, d], sum_send.at[4 * n + d], sum_recv.at[4 * n + d], ((x + d) % 4, s, tp))
            for d in (1, 2, 3)
        ]

    def scale_of(n):
        total = (sums[n, 0] + sums[n, 1]) + (sums[n, 2] + sums[n, 3])
        return to_column(lax.rsqrt(total / HW + EPS))

    normalize()
    relay(4)
    relay(0)
    arrive(4)
    arrive(0)
    g0, g1, g2 = parts
    g0.begin()
    send_tokens()
    g0.first_near(3)
    g0.first_near(1)
    g0.second_near(0)
    g0.first_far()
    relay(1)
    g0.second_near(3)
    arrive(1)
    g1.begin()
    g0.second_near(1)
    g1.first_near(3)
    g1.first_near(1)
    g0.second_near(2)
    g1.second_near(0)
    g1.first_far()
    relay(2)
    for k in (0, 3, 1, 2):
        g0.second_far(k)
    pass_tokens(0)
    g1.second_near(3)
    arrive(2)
    g2.begin()
    g1.second_near(1)
    g2.first_near(3)
    g2.first_near(1)
    pass_tokens(1)
    g1.second_near(2)
    g2.second_near(0)
    g2.first_far()
    for k in (0, 3, 1, 2):
        g1.second_far(k)
    g2.second_near(3)
    pass_tokens(2)
    g2.second_near(1)
    pass_tokens(3)
    siblings(0)
    need_tokens()
    dots(0)
    sums[0, 0] = row_sum(1)
    g2.second_near(2)

    partner = (x, s + 1 - 2 * yh, tp)
    z_up, z_down = (x, ((z + 1) % 4) * 2 + yh, tp), (x, ((z + 3) % 4) * 2 + yh, tp)
    other = 1 - yh

    def wo_copy(i, z2, yh2, device):
        return remote(wo_place(z2, yh2), wo_place(z2, yh2), wo_send.at[i], wo_recv.at[i], device)

    z_prev, z_next, z_far = (z + 3) % 4, (z + 1) % 4, (z + 2) % 4
    relay(3)
    arrive(3)
    wo_steps = [wo_copy(0, z, yh, partner), wo_copy(1, z, yh, z_up), wo_copy(2, z, yh, z_down)]
    for copy in wo_steps:
        copy.start()

    siblings(1)
    key_shares = share(0)
    for copy in key_shares:
        copy.start()

    def wo_more(copy):
        copy.start()
        wo_steps.append(copy)

    wo_copy(0, z, other, partner).wait_recv()
    wo_more(wo_copy(3, z, other, z_up))
    wo_more(wo_copy(4, z, other, z_down))
    dots(1)
    kv_out[:, COLS:] = acc[2].astype(jnp.bfloat16)
    wo_copy(1, z_prev, yh, partner).wait_recv()
    wo_more(wo_copy(5, z_prev, yh, z_up))
    for copy in key_shares:
        copy.wait()
    gains = gain[...].astype(jnp.float32)
    kv_out[:, :COLS] = (acc[1] * scale_of(0) * gains[1:2]).astype(jnp.bfloat16)
    for k in (0, 3, 1, 2):
        g2.second_far(k)
    wo_copy(4, z_next, other, partner).wait_recv()
    wo_more(wo_copy(6, z_next, other, z_down))
    siblings(2)
    dots(2)
    sums[1, 0] = row_sum(0)
    wo_copy(2, z_next, yh, partner).wait_recv()
    wo_copy(3, z_prev, other, partner).wait_recv()
    query_shares = share(1)
    for copy in query_shares:
        copy.start()
    for gather in parts:
        gather.finish()

    @pl.when(x == root)
    def _():
        for group in range(4):
            pl.when(tp == group)(lambda group=group: root_copies(group, drain))

    @pl.when(x == mid)
    def _():
        for i in range(5):
            mid_copy(i)[1].wait_send()

    @pl.when(turn_of == 0)
    def _():
        for i in range(4):
            x_copy(i, 0, up).wait_send()
            x_copy(i, 1, down).wait_send()

    @pl.when(forward)
    def _():
        for i in range(4):
            x_copy(i, 0, onward).wait_send()

    for copy in query_shares:
        copy.wait()
    q_out[...] = (acc[0] * scale_of(1) * gains[0:1]).astype(jnp.bfloat16)
    wo_copy(5, z_far, yh, partner).wait_recv()
    wo_copy(6, z_far, other, partner).wait_recv()
    for copy in wo_steps:
        copy.wait_send()


def qkv_call(root, w, wo, gain, x, mod):
    return pl.pallas_call(
        lambda *refs: qkv_kernel(root, *refs),
        out_shape=[
            jax.ShapeDtypeStruct((ROWS, COLS), jnp.bfloat16),
            jax.ShapeDtypeStruct((ROWS, 2 * COLS), jnp.bfloat16),
            jax.ShapeDtypeStruct((COLS, 2 * COLS), jnp.bfloat16),
        ],
        in_specs=[ANY, ANY, ANY, ANY, VMEM],
        out_specs=[VMEM, VMEM, ANY],
        scratch_shapes=[
            pltpu.VMEM((3, 8, COLS, COLS), jnp.bfloat16),
            pltpu.VMEM((ROWS, D), jnp.bfloat16),
            pltpu.VMEM((ROWS, D), jnp.bfloat16),
            pltpu.VMEM((3, ROWS, COLS), jnp.float32),
            pltpu.VMEM((2, 4, 8, ROWS), jnp.float32),
            pltpu.VMEM((16, COLS), jnp.bfloat16),
            pltpu.VMEM((3, QUARTER, COLS), jnp.bfloat16),
            pltpu.VMEM((QUARTER, COLS), jnp.bfloat16),
            pltpu.VMEM((16, COLS), jnp.bfloat16),
            *gather_sems(3),
            pltpu.SemaphoreType.DMA((20,)),
            pltpu.SemaphoreType.DMA((5,)),
            pltpu.SemaphoreType.DMA((5,)),
            pltpu.SemaphoreType.DMA((5,)),
            pltpu.SemaphoreType.DMA((5,)),
            pltpu.SemaphoreType.DMA((8,)),
            pltpu.SemaphoreType.DMA((4,)),
            pltpu.SemaphoreType.DMA((5,)),
            pltpu.SemaphoreType.DMA((7,)),
            pltpu.SemaphoreType.DMA((7,)),
            pltpu.SemaphoreType.DMA((8,)),
            pltpu.SemaphoreType.DMA((8,)),
        ],
        compiler_params=pltpu.CompilerParams(has_side_effects=True, vmem_limit_bytes=LIMIT, collective_id=1 + root),
        name=f"qkv_{root}",
    )(w, wo, gain, x, mod)


ARRIVAL = [
    (0, 0, 0), (0, 3, 0), (0, 1, 0), (1, 0, 0),
    (0, 0, 3), (0, 0, 1), (1, 3, 0), (1, 1, 0),
    (0, 2, 0), (0, 3, 3), (0, 3, 1), (1, 0, 3),
    (1, 0, 1), (1, 2, 0), (1, 3, 3), (1, 3, 1),
    (0, 0, 2), (0, 1, 3), (0, 1, 1), (1, 0, 2),
    (1, 1, 3), (1, 1, 1), (0, 3, 2), (1, 3, 2),
    (0, 2, 3), (0, 2, 1), (1, 2, 3), (1, 2, 1),
    (0, 1, 2), (0, 2, 2), (1, 1, 2), (1, 2, 2),
]


def attend_kernel(q_ref, kv_ref, wo_ref, x_ref, policy_ref, mod_ref, block_out, err_out,
                  inputs_ref, gate_ref, kvbuf, wofull, acc, top, low, attn, pair_attn, afull, proj, errs,
                  send_sem, recv_sem, pair_sem, wo_send, wo_recv, local_sem,
                  a_send, a_recv, a_pair_send, a_pair_recv, y_send, y_recv, e_send, e_recv):
    x, s, tp = place()
    core = tp % 2
    share_cols = pl.ds(pl.multiple_of(tp * (D // 4), 128), D // 4)
    own_inputs = pltpu.make_async_copy(x_ref.at[:, share_cols], inputs_ref, local_sem.at[6])
    own_gate = pltpu.make_async_copy(mod_ref.at[:, share_cols], gate_ref, local_sem.at[7])
    own_inputs.start()
    own_gate.start()
    greet(neighbours() + [(x, s, 3 - tp)])

    def slot(pair, k, j):
        return kvbuf.at[ARRIVAL.index((pair, k, j))]

    def dest(pair, k, j, k2, j2):
        return kvbuf.at[ARRIVAL.index((pair, k2, j2))]

    def half(ref, h):
        return ref.at[pl.ds(h * (ROWS // 2), ROWS // 2), :]

    gather = Gather(kv_ref, slot, dest, half, send_sem, recv_sem, pair_sem)
    gather.begin()
    own_kv = pltpu.make_async_copy(kv_ref, slot(0, 0, 0), local_sem.at[0])
    own_kv.start()

    up, down = ((x + 1) % 4, s, tp), ((x + 3) % 4, s, tp)
    rows = [pl.ds(0, COLS // 2), pl.ds(COLS // 2, COLS // 2)]

    def wo_copy(i, src, plane, h, device, n):
        return remote(src, wofull.at[plane, rows[h]], wo_send.at[i], wo_recv.at[n], device)

    own_sends = [
        wo_copy(0, wo_ref.at[rows[0]], x, 0, up, 0),
        wo_copy(1, wo_ref.at[rows[1]], x, 1, down, 1),
        wo_copy(2, wo_ref.at[rows[1]], x, 1, up, 2),
        wo_copy(3, wo_ref.at[rows[0]], x, 0, down, 3),
    ]
    for copy in own_sends:
        copy.start()
    own_wo = pltpu.make_async_copy(wo_ref, wofull.at[x], local_sem.at[1])
    own_wo.start()
    below, above, across = (x + 3) % 4, (x + 1) % 4, (x + 2) % 4
    onward = [
        wo_copy(4, wofull.at[below, rows[0]], below, 0, up, 4),
        wo_copy(5, wofull.at[above, rows[1]], above, 1, down, 5),
    ]

    def pass_wo():
        wo_copy(4, wofull.at[below, rows[0]], below, 0, up, 0).wait_recv()
        onward[0].start()
        wo_copy(5, wofull.at[above, rows[1]], above, 1, down, 1).wait_recv()
        onward[1].start()

    def need_wo():
        own_wo.wait()
        wo_copy(2, wo_ref.at[rows[1]], below, 1, up, 2).wait_recv()
        wo_copy(3, wo_ref.at[rows[0]], above, 0, up, 3).wait_recv()
        wo_copy(4, wo_ref.at[rows[0]], across, 0, up, 4).wait_recv()
        wo_copy(5, wo_ref.at[rows[1]], across, 1, up, 5).wait_recv()

    acc[...] = jnp.zeros_like(acc)
    low[...] = jnp.zeros_like(low)
    top[...] = jnp.full_like(top, -1e30)
    factor = float(HD) ** -0.5 * 1.4426950408889634

    def step(h, block):
        cols = pl.ds(pl.multiple_of(h * HD, HD), HD)
        vcols = pl.ds(pl.multiple_of(COLS + h * HD, HD), HD)
        keys = kvbuf[4 * block : 4 * block + 4, :, cols].reshape(4 * ROWS, HD)
        values = kvbuf[4 * block : 4 * block + 4, :, vcols].reshape(4 * ROWS, HD)
        scores = lax.dot_general(
            q_ref[:, cols], keys, (((1,), (1,)), ((), ())), preferred_element_type=jnp.float32
        )
        old = top[h]
        new = jnp.maximum(old, jnp.max(scores, axis=1, keepdims=True))
        top[h] = new
        decay = jnp.exp2((old - new) * factor)
        probs = jnp.exp2((scores - new[:, 0:1]) * factor)
        part = probs[:, 0:128]
        for i in range(1, 4 * ROWS // 128):
            part = part + probs[:, i * 128 : (i + 1) * 128]
        low[h] = low[h] * decay + part
        acc[h] = acc[h] * decay + jnp.dot(probs.astype(jnp.bfloat16), values, preferred_element_type=jnp.float32)

    def flash(block):
        for pair, k, j in ARRIVAL[4 * block : 4 * block + 4]:
            if pair:
                gather.from_sibling(k, j)

        def body(h, carry):
            step(h, block)
            return carry

        lax.fori_loop(0, HEADS_HERE, body, 0)

    gather.first_near(3)
    gather.first_near(1)
    gather.second_near(0)
    gather.first_far()
    own_kv.wait()
    flash(0)
    gather.second_near(3)
    flash(1)
    pass_wo()
    gather.second_near(1)
    flash(2)
    gather.second_far(0)
    flash(3)
    flash(4)
    gather.second_near(2)
    gather.second_far(3)
    flash(5)
    flash(6)
    gather.second_far(1)
    gather.second_far(2)
    for pair, k, j in ARRIVAL[28:]:
        if pair:
            gather.from_sibling(k, j)

    partner = (tp + 2) % 4
    sibling = (x, s, tp + 1 - 2 * core)
    mine = x % 2 == core
    spans = [pl.ds(0, 3 * HD), pl.ds(3 * HD, 2 * HD)]

    def swap(g):
        return remote(attn.at[:, spans[g]], pair_attn.at[:, spans[g]], y_send.at[g], y_recv.at[g], (x, s, partner))

    def near(i, g):
        held = (attn, pair_attn)[i]
        return pltpu.make_async_copy(held.at[:, spans[g]], afull.at[x, :, spans[g]], local_sem.at[2 + 2 * i + g])

    def away(i, g, plane):
        held = (attn, pair_attn)[i]
        return remote(
            held.at[:, spans[g]], afull.at[plane, :, spans[g]], a_send.at[2 * i + g], a_recv.at[2 * plane + g],
            ((tp, partner)[i], s, tp),
        )

    def deliver(i, g):
        block = (tp, partner)[i]

        @pl.when(x == block)
        def _():
            near(i, g).start()

        @pl.when(x != block)
        def _():
            away(i, g, x).start()

    def pair_copy(g, d):
        ref = afull.at[(x + d) % 4, :, spans[g]]
        return remote(ref, ref, a_pair_send.at[4 * g + d], a_pair_recv.at[4 * g + d], sibling)

    def collect(g, d):
        @pl.when(mine)
        def _():
            if d == 0:
                @pl.when(x == tp)
                def _():
                    near(0, g).wait()

                @pl.when(x != tp)
                def _():
                    near(1, g).wait()
            else:
                away(0, g, (x + d) % 4).wait_recv()
            pair_copy(g, d).start()

        @pl.when(jnp.logical_not(mine))
        def _():
            pair_copy(g, d).wait_recv()

    def last(h, carry):
        step(h, 7)
        total = jnp.sum(low[h], axis=1, keepdims=True)
        attn[:, pl.ds(pl.multiple_of(h * HD, HD), HD)] = (acc[h] / total).astype(jnp.bfloat16)

        @pl.when(h == 3)
        def _():
            swap(0).start()
            deliver(0, 0)

        return carry

    lax.fori_loop(0, HEADS_HERE, last, 0)
    need_wo()
    swap(1).start()
    deliver(0, 1)
    swap(0).wait_recv()
    deliver(1, 0)

    def project(g, d):
        plane = (x + d) % 4
        first, count = ((0, 3 * HD), (3 * HD, 2 * HD))[g]
        return jnp.dot(
            afull[plane, :, first : first + count], wofull[plane, first : first + count, :],
            preferred_element_type=jnp.float32,
        )

    swap(1).wait_recv()
    deliver(1, 1)
    for d in (0, 1, 3, 2):
        collect(0, d)
        if d == 0:
            proj[...] = project(0, d)
        else:
            proj[...] += project(0, d)
    for d in (0, 1, 3, 2):
        collect(1, d)
        proj[...] += project(1, d)

    own_inputs.wait()
    own_gate.wait()
    block = (inputs_ref[...].astype(jnp.float32) + gate_ref[2:3] * proj[...]).astype(jnp.bfloat16)
    block_out[...] = block
    differ = block.astype(jnp.float32) - policy_ref[...].astype(jnp.float32)
    errs[0] = to_row(jnp.sum(differ * differ, axis=1, keepdims=True))
    for i in range(2):
        for g in range(2):
            @pl.when(x != (tp, partner)[i])
            def _(i=i, g=g):
                away(i, g, x).wait_send()
    for g in range(2):
        swap(g).wait_send()

    @pl.when(mine)
    def _():
        for g in range(2):
            for d in range(4):
                pair_copy(g, d).wait_send()

    shares = [remote(errs.at[0], errs.at[d], e_send.at[d], e_recv.at[d], (x, s, (tp + d) % 4)) for d in (1, 2, 3)]
    for share in shares:
        share.start()
    for copy in own_sends + onward:
        copy.wait_send()
    gather.finish()
    for share in shares:
        share.wait()
    err_out[...] = ((errs[0] + errs[1]) + (errs[2] + errs[3])) / D


def attend_call(q, kv, wo, x, policy, mod):
    return pl.pallas_call(
        attend_kernel,
        out_shape=[
            jax.ShapeDtypeStruct((ROWS, D // 4), jnp.bfloat16),
            jax.ShapeDtypeStruct((8, ROWS), jnp.float32),
        ],
        in_specs=[VMEM, ANY, ANY, ANY, VMEM, ANY],
        out_specs=[VMEM, VMEM],
        scratch_shapes=[
            pltpu.VMEM((ROWS, D // 4), jnp.bfloat16),
            pltpu.VMEM((8, D // 4), jnp.float32),
            pltpu.VMEM((32, ROWS, 2 * COLS), jnp.bfloat16),
            pltpu.VMEM((4, COLS, 2 * COLS), jnp.bfloat16),
            pltpu.VMEM((HEADS_HERE, ROWS, HD), jnp.float32),
            pltpu.VMEM((HEADS_HERE, ROWS, HD), jnp.float32),
            pltpu.VMEM((HEADS_HERE, ROWS, HD), jnp.float32),
            pltpu.VMEM((ROWS, COLS), jnp.bfloat16),
            pltpu.VMEM((ROWS, COLS), jnp.bfloat16),
            pltpu.VMEM((4, ROWS, COLS), jnp.bfloat16),
            pltpu.VMEM((ROWS, D // 4), jnp.float32),
            pltpu.VMEM((4, 8, ROWS), jnp.float32),
            *gather_sems(1),
            pltpu.SemaphoreType.DMA((6,)),
            pltpu.SemaphoreType.DMA((6,)),
            pltpu.SemaphoreType.DMA((8,)),
            pltpu.SemaphoreType.DMA((4,)),
            pltpu.SemaphoreType.DMA((8,)),
            pltpu.SemaphoreType.DMA((8,)),
            pltpu.SemaphoreType.DMA((8,)),
            pltpu.SemaphoreType.DMA((2,)),
            pltpu.SemaphoreType.DMA((2,)),
            pltpu.SemaphoreType.DMA((4,)),
            pltpu.SemaphoreType.DMA((4,)),
        ],
        compiler_params=pltpu.CompilerParams(has_side_effects=True, vmem_limit_bytes=LIMIT, collective_id=5),
        name="attend",
    )(q, kv, wo, x, policy, mod)


def local(latents, policy_out, w_qkv, w_out, qk_gains, mod_table, timestep, owner):
    held = w_qkv.shape[0]
    local_block = owner[0] % held
    root_group = owner[0] // held
    mine_qkv = lax.dynamic_index_in_dim(w_qkv.transpose(0, 2, 1, 3), local_block, 0, keepdims=False)
    mine_out = lax.dynamic_index_in_dim(w_out, local_block, 0, keepdims=False)
    mine_gains = lax.dynamic_index_in_dim(qk_gains, local_block, 0, keepdims=False)
    mine_gains = jnp.pad(mine_gains, ((0, 14), (0, 0)))
    onehot = (jnp.arange(mod_table.shape[0], dtype=jnp.int32) == timestep[0]).astype(jnp.float32)
    modulation = jnp.tensordot(onehot, mod_table, axes=1, precision=lax.Precision.HIGHEST)
    mod = jnp.pad(modulation, ((0, 5), (0, 0)))
    q, kv, wo_rows = lax.switch(
        root_group,
        [lambda *a, root=root: tuple(qkv_call(root, *a)) for root in range(4)],
        mine_qkv, mine_out, mine_gains, latents[0], mod,
    )
    block, squares = attend_call(q, kv, wo_rows, latents[0], policy_out[0], mod)
    return (block[None], squares[0:1])


def solution(mesh):
    placed = (
        P(None, ("own", "seq"), None),
        P(None, ("own", "seq"), "tp"),
        P("own", "seq", None, "tp"),
        P("own", "tp", "seq"),
        P("own", None, "tp"),
        P(),
        P(),
        P(),
    )
    return jax.shard_map(
        local,
        mesh=mesh,
        in_specs=placed,
        out_specs=(P(None, ("own", "seq"), "tp"), P(None, ("own", "seq"))),
        check_vma=False,
    )
```

```python
import jax
import jax.numpy as jnp
from jax import lax
from jax.experimental import pallas as pl
from jax.experimental.pallas import tpu as pltpu
from jax.sharding import PartitionSpec as P

D = 5120
HD = 128
HW = 2560
ROWS = 256
COLS = 640
HEADS_HERE = 5
QUARTER = 160
EPS = 1e-06
MESH = pl.DeviceIdType.MESH
ANY = pl.BlockSpec(memory_space=pl.ANY)
VMEM = pl.BlockSpec(memory_space=pltpu.VMEM)
LIMIT = 62 * 1024 * 1024


def remote(src, dst, send, recv, device):
    return pltpu.make_async_remote_copy(
        src_ref=src, dst_ref=dst, send_sem=send, recv_sem=recv, device_id=device, device_id_type=MESH
    )


def place():
    x, s, tp = lax.axis_index("own"), lax.axis_index("seq"), lax.axis_index("tp")
    return x, s, tp


def greet(devices, extra=None):
    barrier = pltpu.get_barrier_semaphore()
    for device in devices:
        pl.semaphore_signal(barrier, inc=1, device_id=device, device_id_type=MESH)
    if extra is not None:
        extra(barrier)
    pl.semaphore_wait(barrier, len(devices))


def to_row(column):
    return jnp.transpose(jnp.broadcast_to(column, (ROWS, 128)))[0:8]


def to_column(row):
    return jnp.transpose(jnp.broadcast_to(row[0:1], (128, ROWS)))[:, 0:1]


def gather_sems(count):
    return [
        pltpu.SemaphoreType.DMA((36 * count,)),
        pltpu.SemaphoreType.DMA((20 * count,)),
        pltpu.SemaphoreType.DMA((16 * count,)),
    ]


def neighbours():
    x, s, tp = place()
    core, z, y = tp % 2, s // 2, (s % 2) * 2 + tp // 2

    def device(dx, dz, dy):
        y2 = (y + dy) % 4
        return ((x + dx) % 4, ((z + dz) % 4) * 2 + y2 // 2, (y2 % 2) * 2 + core)

    return [
        device(0, 1, 0), device(0, 3, 0), device(0, 0, 1), device(0, 0, 3),
        device(1, 0, 0), device(2, 0, 0), device(3, 0, 0), (x, s, tp + 1 - 2 * core),
    ]


class Gather:
    def __init__(self, own, slot, dest, half, send_sem, recv_sem, pair_sem, turn=0):
        self.x, s, tp = place()
        core, yl = tp % 2, tp // 2
        z, y = s // 2, (s % 2) * 2 + yl
        self.core, self.z, self.y = core, z, y
        self.own, self.slot, self.dest, self.half = own, slot, dest, half
        self.send_sem, self.recv_sem, self.pair_sem = send_sem, recv_sem, pair_sem
        self.sent = []
        self.base = (36 * turn, 20 * turn, 16 * turn)

        def device(dz, dy):
            z2, y2 = (z + dz) % 4, (y + dy) % 4
            return (self.x, z2 * 2 + y2 // 2, (y2 % 2) * 2 + core)

        self.first = {d: device((1 - core) * d, core * d) for d in (1, 3)}
        self.second = {d: device(core * d, (1 - core) * d) for d in (1, 3)}
        self.sibling = (self.x, s, tp + 1 - 2 * core)
        self.recv_index = {(1, 0): 0, (3, 0): 1, (2, 0): 2}
        for k in range(4):
            self.recv_index[(k, 1)] = 4 + 4 * k
            self.recv_index[(k, 3)] = 5 + 4 * k
            self.recv_index[(k, 2)] = 6 + 4 * k

    def push(self, src, dst, recv, device):
        copy = remote(src, dst, self.send_sem.at[self.base[0] + len(self.sent)], recv, device)
        copy.start()
        self.sent.append(copy)

    def to_sibling(self, k, j, src=None):
        src = self.slot(0, k, j) if src is None else src
        self.push(src, self.dest(1, k, j, k, j), self.pair_sem.at[self.base[2] + 4 * k + j], self.sibling)

    def along_second(self, k, src=None):
        src = self.slot(0, k, 0) if src is None else src
        for d in (1, 3):
            j = (0 - d) % 4
            self.push(src, self.dest(0, k, 0, k, j), self.recv_sem.at[self.base[1] + self.recv_index[(k, j)]], self.second[d])

    def begin(self):
        for d in (1, 3):
            k = (0 - d) % 4
            self.push(self.own, self.dest(0, 0, 0, k, 0), self.recv_sem.at[self.base[1] + self.recv_index[(k, 0)]], self.first[d])
        self.along_second(0, self.own)
        self.to_sibling(0, 0, self.own)

    def take(self, ref, sem):
        remote(ref, ref, self.send_sem.at[self.base[0]], sem, self.sibling).wait_recv()

    def first_near(self, k):
        self.take(self.slot(0, k, 0), self.recv_sem.at[self.base[1] + self.recv_index[(k, 0)]])
        h, d = (0, 1) if k == 3 else (1, 3)
        self.push(
            self.half(self.slot(0, k, 0), h), self.half(self.dest(0, k, 0, 2, 0), h),
            self.recv_sem.at[self.base[1] + self.recv_index[(2, 0)] + h], self.first[d],
        )
        self.along_second(k)
        self.to_sibling(k, 0)

    def first_far(self):
        for h in range(2):
            self.take(self.half(self.slot(0, 2, 0), h), self.recv_sem.at[self.base[1] + self.recv_index[(2, 0)] + h])
        self.along_second(2)
        self.to_sibling(2, 0)

    def second_near(self, k):
        for j in (3, 1):
            self.take(self.slot(0, k, j), self.recv_sem.at[self.base[1] + self.recv_index[(k, j)]])
            h, d = (0, 1) if j == 3 else (1, 3)
            self.push(
                self.half(self.slot(0, k, j), h), self.half(self.dest(0, k, j, k, 2), h),
                self.recv_sem.at[self.base[1] + self.recv_index[(k, 2)] + h], self.second[d],
            )
            self.to_sibling(k, j)

    def second_far(self, k):
        for h in range(2):
            self.take(self.half(self.slot(0, k, 2), h), self.recv_sem.at[self.base[1] + self.recv_index[(k, 2)] + h])
        self.to_sibling(k, 2)

    def from_sibling(self, k, j):
        self.take(self.slot(1, k, j), self.pair_sem.at[self.base[2] + 4 * k + j])

    def finish(self):
        for copy in self.sent:
            copy.wait_send()


ORDER = (1, 2, 0)


def qkv_kernel(root, w_ref, wo_ref, gain_ref, x_ref, mod_ref, q_out, kv_out, wo_out,
               wbuf, xbuf, xraw, acc, sums, gain, w_mid, wo_mid, gain_mid,
               send_sem, recv_sem, pair_sem, spread_send, spread_recv, mid_recv, mid_send, spread_local,
               x_send, x_recv, x_local, wo_send, wo_recv, sum_send, sum_recv):
    x, s, tp = place()
    core = tp % 2
    z, yh = s // 2, s % 2
    y = yh * 2 + tp // 2
    a0 = z * (1 - core) + y * core
    b0 = z * core + y * (1 - core)
    far = (root + 2) % 4
    mid = (root + 3) % 4 if ((far ^ 1) - root) % 4 == 1 else (root + 1) % 4

    turn_of = (x - tp) % 4

    raw = pltpu.make_async_copy(x_ref, xraw, x_local.at[4])

    @pl.when(turn_of == 0)
    def _():
        raw.start()

    barrier = pltpu.get_barrier_semaphore()
    near = neighbours() + [(x, s + 1 - 2 * yh, tp)]
    for device in near:
        pl.semaphore_signal(barrier, inc=1, device_id=device, device_id_type=MESH)
    for group in range(4):
        @pl.when(jnp.logical_not((x == root) & (tp == group)))
        def _(group=group):
            pl.semaphore_signal(barrier, inc=1, device_id=(root, s, group), device_id_type=MESH)

        @pl.when(jnp.logical_not((x == root) & (tp == group) & (z == tp)))
        def _(group=group):
            pl.semaphore_signal(barrier, inc=1, device_id=(root, tp * 2 + yh, group), device_id_type=MESH)

    greeted = jnp.where(x == root, jnp.where(z == tp, 30, 31), 0)
    pl.semaphore_wait(barrier, len(near) + greeted)

    def quarter_of(ref, j, quarter):
        return ref.at[j, pl.ds(quarter * QUARTER, QUARTER), :]

    def w_place(j, quarter):
        return wbuf.at[j, s, pl.ds(quarter * QUARTER, QUARTER), :]

    def wo_place(z2, yh2):
        return wo_out.at[pl.ds(pl.multiple_of(z2 * QUARTER, 32), QUARTER), pl.ds(pl.multiple_of(yh2 * COLS, 128), COLS)]

    def root_copies(group, act):
        plane = mid if group == far else group
        through = group == far
        sems = mid_recv if through else spread_recv
        for c, j in enumerate(ORDER):
            for quarter in range(4):
                piece = quarter_of(w_ref, j, quarter)
                land = w_mid.at[c] if through else w_place(j, quarter)
                if plane == root and quarter == group:
                    act(pltpu.make_async_copy(piece, land, spread_local.at[c]), True)
                else:
                    act(remote(piece, land, spread_send.at[4 * c + quarter], sems.at[c], (plane, s, quarter)), False)
                if c == 0:
                    land = gain_mid if through else gain
                    if plane == root and quarter == group:
                        act(pltpu.make_async_copy(gain_ref, land, spread_local.at[4]), True)
                    else:
                        act(remote(gain_ref, land, spread_send.at[16 + quarter], sems.at[4], (plane, s, quarter)), False)

    def root_wo(group, act):
        plane = mid if group == far else group
        through = group == far
        sems = mid_recv if through else spread_recv
        for quarter in range(4):
            piece = wo_ref.at[pl.ds(quarter * QUARTER, QUARTER), :]
            land = wo_mid if through else wo_place(quarter, yh)

            def go(piece=piece, land=land, quarter=quarter):
                act(remote(piece, land, spread_send.at[12 + quarter], sems.at[3], (plane, quarter * 2 + yh, z)), False)

            if plane == root:
                here = (z == group) & (z == quarter)

                @pl.when(here)
                def _(piece=piece, land=land):
                    act(pltpu.make_async_copy(piece, land, spread_local.at[3]), True)

                pl.when(jnp.logical_not(here))(go)
            else:
                go()

    def start(copy, here):
        copy.start()

    def drain(copy, here):
        if not here:
            copy.wait_send()

    def at_root(copies, act):
        @pl.when(x == root)
        def _():
            for group in range(4):
                pl.when(tp == group)(lambda group=group: copies(group, act))

    at_root(root_copies, start)

    def mid_copy(i):
        held = (w_mid.at[0], w_mid.at[1], w_mid.at[2], wo_mid, gain_mid)[i]
        if i < 3:
            land = wbuf.at[ORDER[i], s, pl.ds(pl.multiple_of(tp * QUARTER, 32), QUARTER), :]
        else:
            land = (wo_place(z, yh), gain)[i - 3]
        return remote(held, held, mid_send.at[i], mid_recv.at[i], (far, s, tp)), remote(
            held, land, mid_send.at[i], spread_recv.at[i], (far, s, tp)
        )

    def relay(i):
        @pl.when(x == mid)
        def _():
            arrived, hop = mid_copy(i)
            arrived.wait_recv()
            hop.start()

    def own_place(i):
        if i < 3:
            return wbuf.at[ORDER[i], s, pl.ds(pl.multiple_of(tp * QUARTER, 32), QUARTER), :]
        return (wo_place(z, yh), gain)[i - 3]

    def arrive(i):
        ref = own_place(i)
        here = (x == root) & (tp == root)
        if i == 3:
            here = here & (z == root)

        @pl.when(here)
        def _():
            pltpu.make_async_copy(ref, ref, spread_local.at[i]).wait()

        @pl.when(jnp.logical_not(here))
        def _():
            remote(ref, ref, spread_send.at[0], spread_recv.at[i], (x, s, tp)).wait_recv()

    def chunk(c):
        j = ORDER[c]

        def slot(pair, k, m):
            if pair:
                a, b, kind = (b0 + k) % 4, (a0 + m) % 4, 1 - core
            else:
                a, b, kind = (a0 + k) % 4, (b0 + m) % 4, core
            z2 = a * (1 - kind) + b * kind
            y2 = a * kind + b * (1 - kind)
            offset = pl.multiple_of(((y2 % 2) * 2 + kind) * QUARTER, 32)
            return wbuf.at[j, z2 * 2 + y2 // 2, pl.ds(offset, QUARTER), :]

        def dest(pair, k, m, k2, m2):
            return slot(0, k, m)

        def half(ref, h):
            return ref.at[pl.ds(h * (QUARTER // 2), QUARTER // 2), :]

        return Gather(slot(0, 0, 0), slot, dest, half, send_sem, recv_sem, pair_sem, c)

    parts = [chunk(c) for c in range(3)]

    part = [pl.ds(i * D // 4, D // 4) for i in range(4)]
    up, down = ((x + 1) % 4, s, tp), ((x + 3) % 4, s, tp)
    forward = turn_of == 3 - 2 * core
    onward = ((x + 3 + 2 * core) % 4, s, tp)

    def x_copy(i, n, device):
        return remote(xbuf.at[:, part[i]], xbuf.at[:, part[i]], x_send.at[4 * n + i], x_recv.at[i], device)

    def normalize():
        @pl.when(turn_of == 0)
        def _():
            raw.wait()
            shift, scale = mod_ref[0:1], 1.0 + mod_ref[1:2]

            def body(i, carry):
                at = pl.ds(pl.multiple_of(i * 16, 16), 16)
                inputs = xraw[at].astype(jnp.float32)
                center = jnp.mean(inputs, axis=-1, keepdims=True)
                spread = jnp.mean((inputs - center) ** 2, axis=-1, keepdims=True)
                normed = (inputs - center) * lax.rsqrt(spread + EPS)
                xbuf[at] = (normed * scale + shift).astype(jnp.bfloat16)
                return carry

            lax.fori_loop(0, ROWS // 16, body, 0)

    def send_tokens(now):
        @pl.when((turn_of == 0) & now)
        def _():
            for i in range(4):
                x_copy(i, 0, up).start()
                x_copy(i, 1, down).start()

    def pass_tokens(i):
        @pl.when(forward)
        def _():
            x_copy(i, 0, onward).wait_recv()
            x_copy(i, 0, onward).start()

    def need_tokens(i):
        @pl.when((turn_of != 0) & jnp.logical_not(forward))
        def _():
            x_copy(i, 0, up).wait_recv()

    def dots(c, first, stop):
        j = ORDER[c]

        def body(row, carry):
            tokens = xbuf[:, pl.ds(pl.multiple_of(row * COLS, 128), COLS)]
            acc[j] += jnp.dot(tokens, wbuf[j, row], preferred_element_type=jnp.float32)
            return carry

        lax.fori_loop(first, stop, body, 0)

    def siblings(c):
        for k in range(4):
            for m in range(4):
                parts[c].from_sibling(k, m)

    def row_sum(j):
        return to_row(jnp.sum(acc[j] * acc[j], axis=1, keepdims=True))

    def share(n):
        return [
            remote(sums.at[n, 0], sums.at[n, d], sum_send.at[4 * n + d], sum_recv.at[4 * n + d], ((x + d) % 4, s, tp))
            for d in (1, 2, 3)
        ]

    def scale_of(n):
        total = (sums[n, 0] + sums[n, 1]) + (sums[n, 2] + sums[n, 3])
        return to_column(lax.rsqrt(total / HW + EPS))

    normalize()
    send_tokens(x != root)
    relay(4)
    relay(0)
    arrive(4)
    arrive(0)
    g0, g1, g2 = parts
    g0.begin()
    g0.first_near(3)
    g0.first_near(1)
    g0.second_near(0)
    send_tokens(x == root)
    g0.first_far()
    relay(1)
    g0.second_near(3)
    arrive(1)
    g1.begin()
    g0.second_near(1)
    g1.first_near(3)
    g1.first_near(1)
    pass_tokens(0)
    g0.second_near(2)
    g1.second_near(0)
    g1.first_far()
    relay(2)
    for k in (0, 3, 1, 2):
        g0.second_far(k)
    pass_tokens(1)
    g1.second_near(3)
    arrive(2)
    g2.begin()
    g1.second_near(1)
    g2.first_near(3)
    g2.first_near(1)
    pass_tokens(2)
    g1.second_near(2)
    at_root(root_wo, start)
    g2.second_near(0)
    g2.first_far()
    for k in (0, 3, 1, 2):
        g1.second_far(k)
    acc[...] = jnp.zeros_like(acc)
    pass_tokens(3)
    g2.second_near(3)
    siblings(0)
    for i in (0, 1):
        need_tokens(i)
        dots(0, 2 * i, 2 * i + 2)
    g2.second_near(1)
    need_tokens(2)
    dots(0, 4, 6)
    g2.second_near(2)
    siblings(1)
    dots(1, 0, 6)
    need_tokens(3)
    dots(0, 6, 8)
    sums[0, 0] = row_sum(1)
    dots(1, 6, 8)

    partner = (x, s + 1 - 2 * yh, tp)
    z_up, z_down = (x, ((z + 1) % 4) * 2 + yh, tp), (x, ((z + 3) % 4) * 2 + yh, tp)
    other = 1 - yh

    def wo_copy(i, z2, yh2, device):
        return remote(wo_place(z2, yh2), wo_place(z2, yh2), wo_send.at[i], wo_recv.at[i], device)

    z_prev, z_next, z_far = (z + 3) % 4, (z + 1) % 4, (z + 2) % 4
    wo_steps = []

    def wo_more(copy):
        copy.start()
        wo_steps.append(copy)

    key_shares = share(0)
    for copy in key_shares:
        copy.start()
    kv_out[:, COLS:] = acc[2].astype(jnp.bfloat16)
    for k in (0, 3, 1, 2):
        g2.second_far(k)
    relay(3)
    arrive(3)
    wo_more(wo_copy(0, z, yh, partner))
    wo_more(wo_copy(1, z, yh, z_up))
    wo_more(wo_copy(2, z, yh, z_down))
    for copy in key_shares:
        copy.wait()
    gains = gain[...].astype(jnp.float32)
    kv_out[:, :COLS] = (acc[1] * scale_of(0) * gains[1:2]).astype(jnp.bfloat16)
    siblings(2)
    dots(2, 0, 8)
    sums[1, 0] = row_sum(0)
    wo_copy(0, z, other, partner).wait_recv()
    wo_more(wo_copy(3, z, other, z_up))
    wo_more(wo_copy(4, z, other, z_down))
    wo_copy(1, z_prev, yh, partner).wait_recv()
    wo_more(wo_copy(5, z_prev, yh, z_up))
    query_shares = share(1)
    for copy in query_shares:
        copy.start()
    wo_copy(4, z_next, other, partner).wait_recv()
    wo_more(wo_copy(6, z_next, other, z_down))
    wo_copy(2, z_next, yh, partner).wait_recv()
    wo_copy(3, z_prev, other, partner).wait_recv()
    for gather in parts:
        gather.finish()

    at_root(root_copies, drain)
    at_root(root_wo, drain)

    @pl.when(x == mid)
    def _():
        for i in range(5):
            mid_copy(i)[1].wait_send()

    @pl.when(turn_of == 0)
    def _():
        for i in range(4):
            x_copy(i, 0, up).wait_send()
            x_copy(i, 1, down).wait_send()

    @pl.when(forward)
    def _():
        for i in range(4):
            x_copy(i, 0, onward).wait_send()

    for copy in query_shares:
        copy.wait()
    q_out[...] = (acc[0] * scale_of(1) * gains[0:1]).astype(jnp.bfloat16)
    wo_copy(5, z_far, yh, partner).wait_recv()
    wo_copy(6, z_far, other, partner).wait_recv()
    for copy in wo_steps:
        copy.wait_send()


def qkv_call(root, w, wo, gain, x, mod):
    return pl.pallas_call(
        lambda *refs: qkv_kernel(root, *refs),
        out_shape=[
            jax.ShapeDtypeStruct((ROWS, COLS), jnp.bfloat16),
            jax.ShapeDtypeStruct((ROWS, 2 * COLS), jnp.bfloat16),
            jax.ShapeDtypeStruct((COLS, 2 * COLS), jnp.bfloat16),
        ],
        in_specs=[ANY, ANY, ANY, ANY, VMEM],
        out_specs=[VMEM, VMEM, ANY],
        scratch_shapes=[
            pltpu.VMEM((3, 8, COLS, COLS), jnp.bfloat16),
            pltpu.VMEM((ROWS, D), jnp.bfloat16),
            pltpu.VMEM((ROWS, D), jnp.bfloat16),
            pltpu.VMEM((3, ROWS, COLS), jnp.float32),
            pltpu.VMEM((2, 4, 8, ROWS), jnp.float32),
            pltpu.VMEM((16, COLS), jnp.bfloat16),
            pltpu.VMEM((3, QUARTER, COLS), jnp.bfloat16),
            pltpu.VMEM((QUARTER, COLS), jnp.bfloat16),
            pltpu.VMEM((16, COLS), jnp.bfloat16),
            *gather_sems(3),
            pltpu.SemaphoreType.DMA((20,)),
            pltpu.SemaphoreType.DMA((5,)),
            pltpu.SemaphoreType.DMA((5,)),
            pltpu.SemaphoreType.DMA((5,)),
            pltpu.SemaphoreType.DMA((5,)),
            pltpu.SemaphoreType.DMA((8,)),
            pltpu.SemaphoreType.DMA((4,)),
            pltpu.SemaphoreType.DMA((5,)),
            pltpu.SemaphoreType.DMA((7,)),
            pltpu.SemaphoreType.DMA((7,)),
            pltpu.SemaphoreType.DMA((8,)),
            pltpu.SemaphoreType.DMA((8,)),
        ],
        compiler_params=pltpu.CompilerParams(has_side_effects=True, vmem_limit_bytes=LIMIT, collective_id=1 + root),
        name=f"qkv_{root}",
    )(w, wo, gain, x, mod)


ARRIVAL = [
    (0, 0, 0), (0, 3, 0), (0, 1, 0), (1, 0, 0),
    (0, 0, 3), (0, 0, 1), (1, 3, 0), (1, 1, 0),
    (0, 2, 0), (0, 3, 3), (0, 3, 1), (1, 0, 3),
    (1, 0, 1), (1, 2, 0), (1, 3, 3), (1, 3, 1),
    (0, 0, 2), (0, 1, 3), (0, 1, 1), (1, 0, 2),
    (1, 1, 3), (1, 1, 1), (0, 3, 2), (1, 3, 2),
    (0, 2, 3), (0, 2, 1), (1, 2, 3), (1, 2, 1),
    (0, 1, 2), (0, 2, 2), (1, 1, 2), (1, 2, 2),
]


def attend_kernel(q_ref, kv_ref, wo_ref, x_ref, policy_ref, mod_ref, block_out, err_out,
                  inputs_ref, gate_ref, kvbuf, wofull, acc, top, low, attn, pair_attn, afull, proj, errs,
                  send_sem, recv_sem, pair_sem, wo_send, wo_recv, local_sem,
                  a_send, a_recv, a_pair_send, a_pair_recv, y_send, y_recv, e_send, e_recv):
    x, s, tp = place()
    core = tp % 2
    share_cols = pl.ds(pl.multiple_of(tp * (D // 4), 128), D // 4)
    own_inputs = pltpu.make_async_copy(x_ref.at[:, share_cols], inputs_ref, local_sem.at[6])
    own_gate = pltpu.make_async_copy(mod_ref.at[:, share_cols], gate_ref, local_sem.at[7])
    own_inputs.start()
    own_gate.start()
    greet(neighbours() + [(x, s, 3 - tp)])

    def slot(pair, k, j):
        return kvbuf.at[ARRIVAL.index((pair, k, j))]

    def dest(pair, k, j, k2, j2):
        return kvbuf.at[ARRIVAL.index((pair, k2, j2))]

    def half(ref, h):
        return ref.at[pl.ds(h * (ROWS // 2), ROWS // 2), :]

    gather = Gather(kv_ref, slot, dest, half, send_sem, recv_sem, pair_sem)
    gather.begin()
    own_kv = pltpu.make_async_copy(kv_ref, slot(0, 0, 0), local_sem.at[0])
    own_kv.start()

    up, down = ((x + 1) % 4, s, tp), ((x + 3) % 4, s, tp)
    rows = [pl.ds(0, COLS // 2), pl.ds(COLS // 2, COLS // 2)]

    def wo_copy(i, src, plane, h, device, n):
        return remote(src, wofull.at[plane, rows[h]], wo_send.at[i], wo_recv.at[n], device)

    own_sends = [
        wo_copy(0, wo_ref.at[rows[0]], x, 0, up, 0),
        wo_copy(1, wo_ref.at[rows[1]], x, 1, down, 1),
        wo_copy(2, wo_ref.at[rows[1]], x, 1, up, 2),
        wo_copy(3, wo_ref.at[rows[0]], x, 0, down, 3),
    ]
    for copy in own_sends:
        copy.start()
    own_wo = pltpu.make_async_copy(wo_ref, wofull.at[x], local_sem.at[1])
    own_wo.start()
    below, above, across = (x + 3) % 4, (x + 1) % 4, (x + 2) % 4
    onward = [
        wo_copy(4, wofull.at[below, rows[0]], below, 0, up, 4),
        wo_copy(5, wofull.at[above, rows[1]], above, 1, down, 5),
    ]

    def pass_wo():
        wo_copy(4, wofull.at[below, rows[0]], below, 0, up, 0).wait_recv()
        onward[0].start()
        wo_copy(5, wofull.at[above, rows[1]], above, 1, down, 1).wait_recv()
        onward[1].start()

    def need_wo():
        own_wo.wait()
        wo_copy(2, wo_ref.at[rows[1]], below, 1, up, 2).wait_recv()
        wo_copy(3, wo_ref.at[rows[0]], above, 0, up, 3).wait_recv()
        wo_copy(4, wo_ref.at[rows[0]], across, 0, up, 4).wait_recv()
        wo_copy(5, wo_ref.at[rows[1]], across, 1, up, 5).wait_recv()

    acc[...] = jnp.zeros_like(acc)
    low[...] = jnp.zeros_like(low)
    top[...] = jnp.full_like(top, -1e30)
    factor = float(HD) ** -0.5 * 1.4426950408889634

    def step(h, block):
        cols = pl.ds(pl.multiple_of(h * HD, HD), HD)
        vcols = pl.ds(pl.multiple_of(COLS + h * HD, HD), HD)
        keys = kvbuf[4 * block : 4 * block + 4, :, cols].reshape(4 * ROWS, HD)
        values = kvbuf[4 * block : 4 * block + 4, :, vcols].reshape(4 * ROWS, HD)
        scores = lax.dot_general(
            q_ref[:, cols], keys, (((1,), (1,)), ((), ())), preferred_element_type=jnp.float32
        )
        old = top[h]
        new = jnp.maximum(old, jnp.max(scores, axis=1, keepdims=True))
        top[h] = new
        decay = jnp.exp2((old - new) * factor)
        probs = jnp.exp2((scores - new[:, 0:1]) * factor)
        part = probs[:, 0:128]
        for i in range(1, 4 * ROWS // 128):
            part = part + probs[:, i * 128 : (i + 1) * 128]
        low[h] = low[h] * decay + part
        acc[h] = acc[h] * decay + jnp.dot(probs.astype(jnp.bfloat16), values, preferred_element_type=jnp.float32)

    def flash(block):
        for pair, k, j in ARRIVAL[4 * block : 4 * block + 4]:
            if pair:
                gather.from_sibling(k, j)

        def body(h, carry):
            step(h, block)
            return carry

        lax.fori_loop(0, HEADS_HERE, body, 0)

    gather.first_near(3)
    gather.first_near(1)
    gather.second_near(0)
    gather.first_far()
    own_kv.wait()
    flash(0)
    gather.second_near(3)
    flash(1)
    pass_wo()
    gather.second_near(1)
    flash(2)
    gather.second_far(0)
    flash(3)
    flash(4)
    gather.second_near(2)
    gather.second_far(3)
    flash(5)
    flash(6)
    gather.second_far(1)
    gather.second_far(2)
    for pair, k, j in ARRIVAL[28:]:
        if pair:
            gather.from_sibling(k, j)

    partner = (tp + 2) % 4
    sibling = (x, s, tp + 1 - 2 * core)
    mine = x % 2 == core
    spans = [pl.ds(0, 3 * HD), pl.ds(3 * HD, 2 * HD)]

    def swap(g):
        return remote(attn.at[:, spans[g]], pair_attn.at[:, spans[g]], y_send.at[g], y_recv.at[g], (x, s, partner))

    def near(i, g):
        held = (attn, pair_attn)[i]
        return pltpu.make_async_copy(held.at[:, spans[g]], afull.at[x, :, spans[g]], local_sem.at[2 + 2 * i + g])

    def away(i, g, plane):
        held = (attn, pair_attn)[i]
        return remote(
            held.at[:, spans[g]], afull.at[plane, :, spans[g]], a_send.at[2 * i + g], a_recv.at[2 * plane + g],
            ((tp, partner)[i], s, tp),
        )

    def deliver(i, g):
        block = (tp, partner)[i]

        @pl.when(x == block)
        def _():
            near(i, g).start()

        @pl.when(x != block)
        def _():
            away(i, g, x).start()

    def pair_copy(g, d):
        ref = afull.at[(x + d) % 4, :, spans[g]]
        return remote(ref, ref, a_pair_send.at[4 * g + d], a_pair_recv.at[4 * g + d], sibling)

    def collect(g, d):
        @pl.when(mine)
        def _():
            if d == 0:
                @pl.when(x == tp)
                def _():
                    near(0, g).wait()

                @pl.when(x != tp)
                def _():
                    near(1, g).wait()
            else:
                away(0, g, (x + d) % 4).wait_recv()
            pair_copy(g, d).start()

        @pl.when(jnp.logical_not(mine))
        def _():
            pair_copy(g, d).wait_recv()

    def last(h, carry):
        step(h, 7)
        total = jnp.sum(low[h], axis=1, keepdims=True)
        attn[:, pl.ds(pl.multiple_of(h * HD, HD), HD)] = (acc[h] / total).astype(jnp.bfloat16)

        @pl.when(h == 3)
        def _():
            swap(0).start()
            deliver(0, 0)

        return carry

    lax.fori_loop(0, HEADS_HERE, last, 0)
    need_wo()
    swap(1).start()
    deliver(0, 1)
    swap(0).wait_recv()
    deliver(1, 0)

    def project(g, d):
        plane = (x + d) % 4
        first, count = ((0, 3 * HD), (3 * HD, 2 * HD))[g]
        return jnp.dot(
            afull[plane, :, first : first + count], wofull[plane, first : first + count, :],
            preferred_element_type=jnp.float32,
        )

    swap(1).wait_recv()
    deliver(1, 1)
    for d in (0, 1, 3, 2):
        collect(0, d)
        if d == 0:
            proj[...] = project(0, d)
        else:
            proj[...] += project(0, d)
    for d in (0, 1, 3, 2):
        collect(1, d)
        proj[...] += project(1, d)

    own_inputs.wait()
    own_gate.wait()
    block = (inputs_ref[...].astype(jnp.float32) + gate_ref[2:3] * proj[...]).astype(jnp.bfloat16)
    block_out[...] = block
    differ = block.astype(jnp.float32) - policy_ref[...].astype(jnp.float32)
    errs[0] = to_row(jnp.sum(differ * differ, axis=1, keepdims=True))
    for i in range(2):
        for g in range(2):
            @pl.when(x != (tp, partner)[i])
            def _(i=i, g=g):
                away(i, g, x).wait_send()
    for g in range(2):
        swap(g).wait_send()

    @pl.when(mine)
    def _():
        for g in range(2):
            for d in range(4):
                pair_copy(g, d).wait_send()

    shares = [remote(errs.at[0], errs.at[d], e_send.at[d], e_recv.at[d], (x, s, (tp + d) % 4)) for d in (1, 2, 3)]
    for share in shares:
        share.start()
    for copy in own_sends + onward:
        copy.wait_send()
    gather.finish()
    for share in shares:
        share.wait()
    err_out[...] = ((errs[0] + errs[1]) + (errs[2] + errs[3])) / D


def attend_call(q, kv, wo, x, policy, mod):
    return pl.pallas_call(
        attend_kernel,
        out_shape=[
            jax.ShapeDtypeStruct((ROWS, D // 4), jnp.bfloat16),
            jax.ShapeDtypeStruct((8, ROWS), jnp.float32),
        ],
        in_specs=[VMEM, ANY, ANY, ANY, VMEM, ANY],
        out_specs=[VMEM, VMEM],
        scratch_shapes=[
            pltpu.VMEM((ROWS, D // 4), jnp.bfloat16),
            pltpu.VMEM((8, D // 4), jnp.float32),
            pltpu.VMEM((32, ROWS, 2 * COLS), jnp.bfloat16),
            pltpu.VMEM((4, COLS, 2 * COLS), jnp.bfloat16),
            pltpu.VMEM((HEADS_HERE, ROWS, HD), jnp.float32),
            pltpu.VMEM((HEADS_HERE, ROWS, HD), jnp.float32),
            pltpu.VMEM((HEADS_HERE, ROWS, HD), jnp.float32),
            pltpu.VMEM((ROWS, COLS), jnp.bfloat16),
            pltpu.VMEM((ROWS, COLS), jnp.bfloat16),
            pltpu.VMEM((4, ROWS, COLS), jnp.bfloat16),
            pltpu.VMEM((ROWS, D // 4), jnp.float32),
            pltpu.VMEM((4, 8, ROWS), jnp.float32),
            *gather_sems(1),
            pltpu.SemaphoreType.DMA((6,)),
            pltpu.SemaphoreType.DMA((6,)),
            pltpu.SemaphoreType.DMA((8,)),
            pltpu.SemaphoreType.DMA((4,)),
            pltpu.SemaphoreType.DMA((8,)),
            pltpu.SemaphoreType.DMA((8,)),
            pltpu.SemaphoreType.DMA((8,)),
            pltpu.SemaphoreType.DMA((2,)),
            pltpu.SemaphoreType.DMA((2,)),
            pltpu.SemaphoreType.DMA((4,)),
            pltpu.SemaphoreType.DMA((4,)),
        ],
        compiler_params=pltpu.CompilerParams(has_side_effects=True, vmem_limit_bytes=LIMIT, collective_id=5),
        name="attend",
    )(q, kv, wo, x, policy, mod)


def local(latents, policy_out, w_qkv, w_out, qk_gains, mod_table, timestep, owner):
    held = w_qkv.shape[0]
    local_block = owner[0] % held
    root_group = owner[0] // held
    mine_qkv = lax.dynamic_index_in_dim(w_qkv.transpose(0, 2, 1, 3), local_block, 0, keepdims=False)
    mine_out = lax.dynamic_index_in_dim(w_out, local_block, 0, keepdims=False)
    mine_gains = lax.dynamic_index_in_dim(qk_gains, local_block, 0, keepdims=False)
    mine_gains = jnp.pad(mine_gains, ((0, 14), (0, 0)))
    onehot = (jnp.arange(mod_table.shape[0], dtype=jnp.int32) == timestep[0]).astype(jnp.float32)
    modulation = jnp.tensordot(onehot, mod_table, axes=1, precision=lax.Precision.HIGHEST)
    mod = jnp.pad(modulation, ((0, 5), (0, 0)))
    q, kv, wo_rows = lax.switch(
        root_group,
        [lambda *a, root=root: tuple(qkv_call(root, *a)) for root in range(4)],
        mine_qkv, mine_out, mine_gains, latents[0], mod,
    )
    block, squares = attend_call(q, kv, wo_rows, latents[0], policy_out[0], mod)
    return (block[None], squares[0:1])


def solution(mesh):
    placed = (
        P(None, ("own", "seq"), None),
        P(None, ("own", "seq"), "tp"),
        P("own", "seq", None, "tp"),
        P("own", "tp", "seq"),
        P("own", None, "tp"),
        P(),
        P(),
        P(),
    )
    return jax.shard_map(
        local,
        mesh=mesh,
        in_specs=placed,
        out_specs=(P(None, ("own", "seq"), "tp"), P(None, ("own", "seq"))),
        check_vma=False,
    )
```

```python
import jax
import jax.numpy as jnp
from jax import lax
from jax.experimental import pallas as pl
from jax.experimental.pallas import tpu as pltpu
from jax.sharding import PartitionSpec as P

D = 5120
HD = 128
HW = 2560
ROWS = 256
COLS = 640
HEADS_HERE = 5
QUARTER = 160
EPS = 1e-06
MESH = pl.DeviceIdType.MESH
ANY = pl.BlockSpec(memory_space=pl.ANY)
VMEM = pl.BlockSpec(memory_space=pltpu.VMEM)
LIMIT = 62 * 1024 * 1024


def remote(src, dst, send, recv, device):
    return pltpu.make_async_remote_copy(
        src_ref=src, dst_ref=dst, send_sem=send, recv_sem=recv, device_id=device, device_id_type=MESH
    )


def place():
    x, s, tp = lax.axis_index("own"), lax.axis_index("seq"), lax.axis_index("tp")
    return x, s, tp


def greet(devices, extra=None):
    barrier = pltpu.get_barrier_semaphore()
    for device in devices:
        pl.semaphore_signal(barrier, inc=1, device_id=device, device_id_type=MESH)
    if extra is not None:
        extra(barrier)
    pl.semaphore_wait(barrier, len(devices))


def to_row(column):
    return jnp.transpose(jnp.broadcast_to(column, (ROWS, 128)))[0:8]


def to_column(row):
    return jnp.transpose(jnp.broadcast_to(row[0:1], (128, ROWS)))[:, 0:1]


def gather_sems(count):
    return [
        pltpu.SemaphoreType.DMA((36 * count,)),
        pltpu.SemaphoreType.DMA((20 * count,)),
        pltpu.SemaphoreType.DMA((16 * count,)),
    ]


def neighbours():
    x, s, tp = place()
    core, z, y = tp % 2, s // 2, (s % 2) * 2 + tp // 2

    def device(dx, dz, dy):
        y2 = (y + dy) % 4
        return ((x + dx) % 4, ((z + dz) % 4) * 2 + y2 // 2, (y2 % 2) * 2 + core)

    return [
        device(0, 1, 0), device(0, 3, 0), device(0, 0, 1), device(0, 0, 3),
        device(1, 0, 0), device(2, 0, 0), device(3, 0, 0), (x, s, tp + 1 - 2 * core),
    ]


class Gather:
    def __init__(self, own, slot, dest, half, send_sem, recv_sem, pair_sem, turn=0):
        self.x, s, tp = place()
        core, yl = tp % 2, tp // 2
        z, y = s // 2, (s % 2) * 2 + yl
        self.core, self.z, self.y = core, z, y
        self.own, self.slot, self.dest, self.half = own, slot, dest, half
        self.send_sem, self.recv_sem, self.pair_sem = send_sem, recv_sem, pair_sem
        self.sent = []
        self.base = (36 * turn, 20 * turn, 16 * turn)

        def device(dz, dy):
            z2, y2 = (z + dz) % 4, (y + dy) % 4
            return (self.x, z2 * 2 + y2 // 2, (y2 % 2) * 2 + core)

        self.first = {d: device((1 - core) * d, core * d) for d in (1, 3)}
        self.second = {d: device(core * d, (1 - core) * d) for d in (1, 3)}
        self.sibling = (self.x, s, tp + 1 - 2 * core)
        self.recv_index = {(1, 0): 0, (3, 0): 1, (2, 0): 2}
        for k in range(4):
            self.recv_index[(k, 1)] = 4 + 4 * k
            self.recv_index[(k, 3)] = 5 + 4 * k
            self.recv_index[(k, 2)] = 6 + 4 * k

    def push(self, src, dst, recv, device):
        copy = remote(src, dst, self.send_sem.at[self.base[0] + len(self.sent)], recv, device)
        copy.start()
        self.sent.append(copy)

    def to_sibling(self, k, j, src=None):
        src = self.slot(0, k, j) if src is None else src
        self.push(src, self.dest(1, k, j, k, j), self.pair_sem.at[self.base[2] + 4 * k + j], self.sibling)

    def along_second(self, k, src=None):
        src = self.slot(0, k, 0) if src is None else src
        for d in (1, 3):
            j = (0 - d) % 4
            self.push(src, self.dest(0, k, 0, k, j), self.recv_sem.at[self.base[1] + self.recv_index[(k, j)]], self.second[d])

    def begin(self):
        for d in (1, 3):
            k = (0 - d) % 4
            self.push(self.own, self.dest(0, 0, 0, k, 0), self.recv_sem.at[self.base[1] + self.recv_index[(k, 0)]], self.first[d])
        self.along_second(0, self.own)
        self.to_sibling(0, 0, self.own)

    def take(self, ref, sem):
        remote(ref, ref, self.send_sem.at[self.base[0]], sem, self.sibling).wait_recv()

    def first_near(self, k):
        self.take(self.slot(0, k, 0), self.recv_sem.at[self.base[1] + self.recv_index[(k, 0)]])
        h, d = (0, 1) if k == 3 else (1, 3)
        self.push(
            self.half(self.slot(0, k, 0), h), self.half(self.dest(0, k, 0, 2, 0), h),
            self.recv_sem.at[self.base[1] + self.recv_index[(2, 0)] + h], self.first[d],
        )
        self.along_second(k)
        self.to_sibling(k, 0)

    def first_far(self):
        for h in range(2):
            self.take(self.half(self.slot(0, 2, 0), h), self.recv_sem.at[self.base[1] + self.recv_index[(2, 0)] + h])
        self.along_second(2)
        self.to_sibling(2, 0)

    def second_near(self, k):
        for j in (3, 1):
            self.take(self.slot(0, k, j), self.recv_sem.at[self.base[1] + self.recv_index[(k, j)]])
            h, d = (0, 1) if j == 3 else (1, 3)
            self.push(
                self.half(self.slot(0, k, j), h), self.half(self.dest(0, k, j, k, 2), h),
                self.recv_sem.at[self.base[1] + self.recv_index[(k, 2)] + h], self.second[d],
            )
            self.to_sibling(k, j)

    def second_far(self, k):
        for h in range(2):
            self.take(self.half(self.slot(0, k, 2), h), self.recv_sem.at[self.base[1] + self.recv_index[(k, 2)] + h])
        self.to_sibling(k, 2)

    def from_sibling(self, k, j):
        self.take(self.slot(1, k, j), self.pair_sem.at[self.base[2] + 4 * k + j])

    def finish(self):
        for copy in self.sent:
            copy.wait_send()


ORDER = (1, 2, 0)


def qkv_kernel(root, w_ref, wo_ref, gain_ref, x_ref, mod_ref, q_out, kv_out, wo_out,
               wbuf, xbuf, xraw, acc, sums, gain, w_mid, wo_mid, gain_mid,
               send_sem, recv_sem, pair_sem, spread_send, spread_recv, mid_recv, mid_send, spread_local,
               x_send, x_recv, x_local, wo_send, wo_recv, sum_send, sum_recv):
    x, s, tp = place()
    core = tp % 2
    z, yh = s // 2, s % 2
    y = yh * 2 + tp // 2
    a0 = z * (1 - core) + y * core
    b0 = z * core + y * (1 - core)
    far = (root + 2) % 4
    mid = (root + 3) % 4 if ((far ^ 1) - root) % 4 == 1 else (root + 1) % 4

    turn_of = (x - tp) % 4

    raw = pltpu.make_async_copy(x_ref, xraw, x_local.at[4])

    @pl.when(turn_of == 0)
    def _():
        raw.start()

    barrier = pltpu.get_barrier_semaphore()
    near = neighbours() + [(x, s + 1 - 2 * yh, tp)]
    for device in near:
        pl.semaphore_signal(barrier, inc=1, device_id=device, device_id_type=MESH)
    for group in range(4):
        @pl.when(jnp.logical_not((x == root) & (tp == group)))
        def _(group=group):
            pl.semaphore_signal(barrier, inc=1, device_id=(root, s, group), device_id_type=MESH)

        @pl.when(jnp.logical_not((x == root) & (tp == group) & (z == tp)))
        def _(group=group):
            pl.semaphore_signal(barrier, inc=1, device_id=(root, tp * 2 + yh, group), device_id_type=MESH)

    greeted = jnp.where(x == root, jnp.where(z == tp, 30, 31), 0)
    pl.semaphore_wait(barrier, len(near) + greeted)

    def quarter_of(ref, j, quarter):
        return ref.at[j, pl.ds(quarter * QUARTER, QUARTER), :]

    def w_place(j, quarter):
        return wbuf.at[j, s, pl.ds(quarter * QUARTER, QUARTER), :]

    def wo_place(z2, yh2):
        return wo_out.at[pl.ds(pl.multiple_of(z2 * QUARTER, 32), QUARTER), pl.ds(pl.multiple_of(yh2 * COLS, 128), COLS)]

    def root_copies(group, act):
        plane = mid if group == far else group
        through = group == far
        sems = mid_recv if through else spread_recv
        for c, j in enumerate(ORDER):
            for quarter in range(4):
                piece = quarter_of(w_ref, j, quarter)
                land = w_mid.at[c] if through else w_place(j, quarter)
                if plane == root and quarter == group:
                    act(pltpu.make_async_copy(piece, land, spread_local.at[c]), True)
                else:
                    act(remote(piece, land, spread_send.at[4 * c + quarter], sems.at[c], (plane, s, quarter)), False)
                if c == 0:
                    land = gain_mid if through else gain
                    if plane == root and quarter == group:
                        act(pltpu.make_async_copy(gain_ref, land, spread_local.at[4]), True)
                    else:
                        act(remote(gain_ref, land, spread_send.at[16 + quarter], sems.at[4], (plane, s, quarter)), False)

    def root_wo(group, act):
        plane = mid if group == far else group
        through = group == far
        sems = mid_recv if through else spread_recv
        for quarter in range(4):
            piece = wo_ref.at[pl.ds(quarter * QUARTER, QUARTER), :]
            land = wo_mid if through else wo_place(quarter, yh)

            def go(piece=piece, land=land, quarter=quarter):
                act(remote(piece, land, spread_send.at[12 + quarter], sems.at[3], (plane, quarter * 2 + yh, z)), False)

            if plane == root:
                here = (z == group) & (z == quarter)

                @pl.when(here)
                def _(piece=piece, land=land):
                    act(pltpu.make_async_copy(piece, land, spread_local.at[3]), True)

                pl.when(jnp.logical_not(here))(go)
            else:
                go()

    def start(copy, here):
        copy.start()

    def drain(copy, here):
        if not here:
            copy.wait_send()

    def at_root(copies, act):
        @pl.when(x == root)
        def _():
            for group in range(4):
                pl.when(tp == group)(lambda group=group: copies(group, act))

    at_root(root_copies, start)

    def mid_copy(i):
        held = (w_mid.at[0], w_mid.at[1], w_mid.at[2], wo_mid, gain_mid)[i]
        if i < 3:
            land = wbuf.at[ORDER[i], s, pl.ds(pl.multiple_of(tp * QUARTER, 32), QUARTER), :]
        else:
            land = (wo_place(z, yh), gain)[i - 3]
        return remote(held, held, mid_send.at[i], mid_recv.at[i], (far, s, tp)), remote(
            held, land, mid_send.at[i], spread_recv.at[i], (far, s, tp)
        )

    def relay(i):
        @pl.when(x == mid)
        def _():
            arrived, hop = mid_copy(i)
            arrived.wait_recv()
            hop.start()

    def own_place(i):
        if i < 3:
            return wbuf.at[ORDER[i], s, pl.ds(pl.multiple_of(tp * QUARTER, 32), QUARTER), :]
        return (wo_place(z, yh), gain)[i - 3]

    def arrive(i):
        ref = own_place(i)
        here = (x == root) & (tp == root)
        if i == 3:
            here = here & (z == root)

        @pl.when(here)
        def _():
            pltpu.make_async_copy(ref, ref, spread_local.at[i]).wait()

        @pl.when(jnp.logical_not(here))
        def _():
            remote(ref, ref, spread_send.at[0], spread_recv.at[i], (x, s, tp)).wait_recv()

    def chunk(c):
        j = ORDER[c]

        def slot(pair, k, m):
            if pair:
                a, b, kind = (b0 + k) % 4, (a0 + m) % 4, 1 - core
            else:
                a, b, kind = (a0 + k) % 4, (b0 + m) % 4, core
            z2 = a * (1 - kind) + b * kind
            y2 = a * kind + b * (1 - kind)
            offset = pl.multiple_of(((y2 % 2) * 2 + kind) * QUARTER, 32)
            return wbuf.at[j, z2 * 2 + y2 // 2, pl.ds(offset, QUARTER), :]

        def dest(pair, k, m, k2, m2):
            return slot(0, k, m)

        def half(ref, h):
            return ref.at[pl.ds(h * (QUARTER // 2), QUARTER // 2), :]

        return Gather(slot(0, 0, 0), slot, dest, half, send_sem, recv_sem, pair_sem, c)

    parts = [chunk(c) for c in range(3)]

    part = [pl.ds(i * D // 4, D // 4) for i in range(4)]
    up, down = ((x + 1) % 4, s, tp), ((x + 3) % 4, s, tp)
    forward = turn_of == 3 - 2 * core
    onward = ((x + 3 + 2 * core) % 4, s, tp)

    def x_copy(i, n, device):
        return remote(xbuf.at[:, part[i]], xbuf.at[:, part[i]], x_send.at[4 * n + i], x_recv.at[i], device)

    def normalize():
        @pl.when(turn_of == 0)
        def _():
            raw.wait()
            shift, scale = mod_ref[0:1], 1.0 + mod_ref[1:2]

            def body(i, carry):
                at = pl.ds(pl.multiple_of(i * 16, 16), 16)
                inputs = xraw[at].astype(jnp.float32)
                center = jnp.mean(inputs, axis=-1, keepdims=True)
                spread = jnp.mean((inputs - center) ** 2, axis=-1, keepdims=True)
                normed = (inputs - center) * lax.rsqrt(spread + EPS)
                xbuf[at] = (normed * scale + shift).astype(jnp.bfloat16)
                return carry

            lax.fori_loop(0, ROWS // 16, body, 0)

    def send_tokens(now):
        @pl.when((turn_of == 0) & now)
        def _():
            for i in range(4):
                x_copy(i, 0, up).start()
                x_copy(i, 1, down).start()

    def pass_tokens(i):
        @pl.when(forward)
        def _():
            x_copy(i, 0, onward).wait_recv()
            x_copy(i, 0, onward).start()

    def need_tokens(i):
        @pl.when((turn_of != 0) & jnp.logical_not(forward))
        def _():
            x_copy(i, 0, up).wait_recv()

    def dots(c, first, stop):
        j = ORDER[c]

        def body(row, carry):
            tokens = xbuf[:, pl.ds(pl.multiple_of(row * COLS, 128), COLS)]
            acc[j] += jnp.dot(tokens, wbuf[j, row], preferred_element_type=jnp.float32)
            return carry

        lax.fori_loop(first, stop, body, 0)

    def siblings(c):
        for k in range(4):
            for m in range(4):
                parts[c].from_sibling(k, m)

    def row_sum(j):
        return to_row(jnp.sum(acc[j] * acc[j], axis=1, keepdims=True))

    def share(n):
        return [
            remote(sums.at[n, 0], sums.at[n, d], sum_send.at[4 * n + d], sum_recv.at[4 * n + d], ((x + d) % 4, s, tp))
            for d in (1, 2, 3)
        ]

    def scale_of(n):
        total = (sums[n, 0] + sums[n, 1]) + (sums[n, 2] + sums[n, 3])
        return to_column(lax.rsqrt(total / HW + EPS))

    normalize()
    send_tokens(x != root)
    relay(4)
    relay(0)
    arrive(4)
    arrive(0)
    g0, g1, g2 = parts
    g0.begin()
    g0.first_near(3)
    g0.first_near(1)
    g0.second_near(0)
    send_tokens(x == root)
    g0.first_far()
    relay(1)
    g0.second_near(3)
    arrive(1)
    g1.begin()
    g0.second_near(1)
    g1.first_near(3)
    g1.first_near(1)
    pass_tokens(0)
    g0.second_near(2)
    g1.second_near(0)
    g1.first_far()
    relay(2)
    for k in (0, 3, 1, 2):
        g0.second_far(k)
    pass_tokens(1)
    g1.second_near(3)
    arrive(2)
    g2.begin()
    at_root(root_wo, start)
    g1.second_near(1)
    g2.first_near(3)
    g2.first_near(1)
    pass_tokens(2)
    g1.second_near(2)
    g2.second_near(0)
    g2.first_far()
    for k in (0, 3, 1, 2):
        g1.second_far(k)
    acc[...] = jnp.zeros_like(acc)
    pass_tokens(3)
    g2.second_near(3)
    siblings(0)
    for i in (0, 1):
        need_tokens(i)
        dots(0, 2 * i, 2 * i + 2)
    g2.second_near(1)
    need_tokens(2)
    dots(0, 4, 6)
    g2.second_near(2)
    siblings(1)
    dots(1, 0, 6)
    need_tokens(3)
    dots(0, 6, 8)
    sums[0, 0] = row_sum(1)
    dots(1, 6, 8)

    partner = (x, s + 1 - 2 * yh, tp)
    z_up, z_down = (x, ((z + 1) % 4) * 2 + yh, tp), (x, ((z + 3) % 4) * 2 + yh, tp)
    other = 1 - yh

    def wo_copy(i, z2, yh2, device):
        return remote(wo_place(z2, yh2), wo_place(z2, yh2), wo_send.at[i], wo_recv.at[i], device)

    z_prev, z_next, z_far = (z + 3) % 4, (z + 1) % 4, (z + 2) % 4
    wo_steps = []

    def wo_more(copy):
        copy.start()
        wo_steps.append(copy)

    key_shares = share(0)
    for copy in key_shares:
        copy.start()
    kv_out[:, COLS:] = acc[2].astype(jnp.bfloat16)
    for k in (0, 3, 1, 2):
        g2.second_far(k)
    relay(3)
    arrive(3)
    wo_more(wo_copy(0, z, yh, partner))
    wo_more(wo_copy(1, z, yh, z_up))
    wo_more(wo_copy(2, z, yh, z_down))
    for copy in key_shares:
        copy.wait()
    gains = gain[...].astype(jnp.float32)
    kv_out[:, :COLS] = (acc[1] * scale_of(0) * gains[1:2]).astype(jnp.bfloat16)
    siblings(2)
    dots(2, 0, 8)
    sums[1, 0] = row_sum(0)
    wo_copy(0, z, other, partner).wait_recv()
    wo_more(wo_copy(3, z, other, z_up))
    wo_more(wo_copy(4, z, other, z_down))
    wo_copy(1, z_prev, yh, partner).wait_recv()
    wo_more(wo_copy(5, z_prev, yh, z_up))
    query_shares = share(1)
    for copy in query_shares:
        copy.start()
    wo_copy(4, z_next, other, partner).wait_recv()
    wo_more(wo_copy(6, z_next, other, z_down))
    wo_copy(2, z_next, yh, partner).wait_recv()
    wo_copy(3, z_prev, other, partner).wait_recv()
    for gather in parts:
        gather.finish()

    at_root(root_copies, drain)
    at_root(root_wo, drain)

    @pl.when(x == mid)
    def _():
        for i in range(5):
            mid_copy(i)[1].wait_send()

    @pl.when(turn_of == 0)
    def _():
        for i in range(4):
            x_copy(i, 0, up).wait_send()
            x_copy(i, 1, down).wait_send()

    @pl.when(forward)
    def _():
        for i in range(4):
            x_copy(i, 0, onward).wait_send()

    for copy in query_shares:
        copy.wait()
    q_out[...] = (acc[0] * scale_of(1) * gains[0:1]).astype(jnp.bfloat16)
    wo_copy(5, z_far, yh, partner).wait_recv()
    wo_copy(6, z_far, other, partner).wait_recv()
    for copy in wo_steps:
        copy.wait_send()


def qkv_call(root, w, wo, gain, x, mod):
    return pl.pallas_call(
        lambda *refs: qkv_kernel(root, *refs),
        out_shape=[
            jax.ShapeDtypeStruct((ROWS, COLS), jnp.bfloat16),
            jax.ShapeDtypeStruct((ROWS, 2 * COLS), jnp.bfloat16),
            jax.ShapeDtypeStruct((COLS, 2 * COLS), jnp.bfloat16),
        ],
        in_specs=[ANY, ANY, ANY, ANY, VMEM],
        out_specs=[VMEM, VMEM, ANY],
        scratch_shapes=[
            pltpu.VMEM((3, 8, COLS, COLS), jnp.bfloat16),
            pltpu.VMEM((ROWS, D), jnp.bfloat16),
            pltpu.VMEM((ROWS, D), jnp.bfloat16),
            pltpu.VMEM((3, ROWS, COLS), jnp.float32),
            pltpu.VMEM((2, 4, 8, ROWS), jnp.float32),
            pltpu.VMEM((16, COLS), jnp.bfloat16),
            pltpu.VMEM((3, QUARTER, COLS), jnp.bfloat16),
            pltpu.VMEM((QUARTER, COLS), jnp.bfloat16),
            pltpu.VMEM((16, COLS), jnp.bfloat16),
            *gather_sems(3),
            pltpu.SemaphoreType.DMA((20,)),
            pltpu.SemaphoreType.DMA((5,)),
            pltpu.SemaphoreType.DMA((5,)),
            pltpu.SemaphoreType.DMA((5,)),
            pltpu.SemaphoreType.DMA((5,)),
            pltpu.SemaphoreType.DMA((8,)),
            pltpu.SemaphoreType.DMA((4,)),
            pltpu.SemaphoreType.DMA((5,)),
            pltpu.SemaphoreType.DMA((7,)),
            pltpu.SemaphoreType.DMA((7,)),
            pltpu.SemaphoreType.DMA((8,)),
            pltpu.SemaphoreType.DMA((8,)),
        ],
        compiler_params=pltpu.CompilerParams(has_side_effects=True, vmem_limit_bytes=LIMIT, collective_id=1 + root),
        name=f"qkv_{root}",
    )(w, wo, gain, x, mod)


ARRIVAL = [
    (0, 0, 0), (0, 3, 0), (0, 1, 0), (1, 0, 0),
    (0, 0, 3), (0, 0, 1), (1, 3, 0), (1, 1, 0),
    (0, 2, 0), (0, 3, 3), (0, 3, 1), (1, 0, 3),
    (1, 0, 1), (1, 2, 0), (1, 3, 3), (1, 3, 1),
    (0, 0, 2), (0, 1, 3), (0, 1, 1), (1, 0, 2),
    (1, 1, 3), (1, 1, 1), (0, 3, 2), (1, 3, 2),
    (0, 2, 3), (0, 2, 1), (1, 2, 3), (1, 2, 1),
    (0, 1, 2), (0, 2, 2), (1, 1, 2), (1, 2, 2),
]


def attend_kernel(q_ref, kv_ref, wo_ref, x_ref, policy_ref, mod_ref, block_out, err_out,
                  inputs_ref, gate_ref, kvbuf, wofull, acc, top, low, attn, pair_attn, afull, proj, errs,
                  send_sem, recv_sem, pair_sem, wo_send, wo_recv, local_sem,
                  a_send, a_recv, a_pair_send, a_pair_recv, y_send, y_recv, e_send, e_recv):
    x, s, tp = place()
    core = tp % 2
    share_cols = pl.ds(pl.multiple_of(tp * (D // 4), 128), D // 4)
    own_inputs = pltpu.make_async_copy(x_ref.at[:, share_cols], inputs_ref, local_sem.at[6])
    own_gate = pltpu.make_async_copy(mod_ref.at[:, share_cols], gate_ref, local_sem.at[7])
    own_inputs.start()
    own_gate.start()
    greet(neighbours() + [(x, s, 3 - tp)])

    def slot(pair, k, j):
        return kvbuf.at[ARRIVAL.index((pair, k, j))]

    def dest(pair, k, j, k2, j2):
        return kvbuf.at[ARRIVAL.index((pair, k2, j2))]

    def half(ref, h):
        return ref.at[pl.ds(h * (ROWS // 2), ROWS // 2), :]

    gather = Gather(kv_ref, slot, dest, half, send_sem, recv_sem, pair_sem)
    gather.begin()
    own_kv = pltpu.make_async_copy(kv_ref, slot(0, 0, 0), local_sem.at[0])
    own_kv.start()

    up, down = ((x + 1) % 4, s, tp), ((x + 3) % 4, s, tp)
    rows = [pl.ds(0, COLS // 2), pl.ds(COLS // 2, COLS // 2)]

    def wo_copy(i, src, plane, h, device, n):
        return remote(src, wofull.at[plane, rows[h]], wo_send.at[i], wo_recv.at[n], device)

    own_sends = [
        wo_copy(0, wo_ref.at[rows[0]], x, 0, up, 0),
        wo_copy(1, wo_ref.at[rows[1]], x, 1, down, 1),
        wo_copy(2, wo_ref.at[rows[1]], x, 1, up, 2),
        wo_copy(3, wo_ref.at[rows[0]], x, 0, down, 3),
    ]
    for copy in own_sends:
        copy.start()
    own_wo = pltpu.make_async_copy(wo_ref, wofull.at[x], local_sem.at[1])
    own_wo.start()
    below, above, across = (x + 3) % 4, (x + 1) % 4, (x + 2) % 4
    onward = [
        wo_copy(4, wofull.at[below, rows[0]], below, 0, up, 4),
        wo_copy(5, wofull.at[above, rows[1]], above, 1, down, 5),
    ]

    def pass_wo():
        wo_copy(4, wofull.at[below, rows[0]], below, 0, up, 0).wait_recv()
        onward[0].start()
        wo_copy(5, wofull.at[above, rows[1]], above, 1, down, 1).wait_recv()
        onward[1].start()

    def need_wo():
        own_wo.wait()
        wo_copy(2, wo_ref.at[rows[1]], below, 1, up, 2).wait_recv()
        wo_copy(3, wo_ref.at[rows[0]], above, 0, up, 3).wait_recv()
        wo_copy(4, wo_ref.at[rows[0]], across, 0, up, 4).wait_recv()
        wo_copy(5, wo_ref.at[rows[1]], across, 1, up, 5).wait_recv()

    acc[...] = jnp.zeros_like(acc)
    low[...] = jnp.zeros_like(low)
    top[...] = jnp.full_like(top, -1e30)
    factor = float(HD) ** -0.5 * 1.4426950408889634

    def step(h, block):
        cols = pl.ds(pl.multiple_of(h * HD, HD), HD)
        vcols = pl.ds(pl.multiple_of(COLS + h * HD, HD), HD)
        keys = kvbuf[4 * block : 4 * block + 4, :, cols].reshape(4 * ROWS, HD)
        values = kvbuf[4 * block : 4 * block + 4, :, vcols].reshape(4 * ROWS, HD)
        scores = lax.dot_general(
            q_ref[:, cols], keys, (((1,), (1,)), ((), ())), preferred_element_type=jnp.float32
        )
        old = top[h]
        new = jnp.maximum(old, jnp.max(scores, axis=1, keepdims=True))
        top[h] = new
        decay = jnp.exp2((old - new) * factor)
        probs = jnp.exp2((scores - new[:, 0:1]) * factor)
        part = probs[:, 0:128]
        for i in range(1, 4 * ROWS // 128):
            part = part + probs[:, i * 128 : (i + 1) * 128]
        low[h] = low[h] * decay + part
        acc[h] = acc[h] * decay + jnp.dot(probs.astype(jnp.bfloat16), values, preferred_element_type=jnp.float32)

    def flash(block):
        for pair, k, j in ARRIVAL[4 * block : 4 * block + 4]:
            if pair:
                gather.from_sibling(k, j)

        def body(h, carry):
            step(h, block)
            return carry

        lax.fori_loop(0, HEADS_HERE, body, 0)

    gather.first_near(3)
    gather.first_near(1)
    gather.second_near(0)
    gather.first_far()
    own_kv.wait()
    flash(0)
    gather.second_near(3)
    flash(1)
    pass_wo()
    gather.second_near(1)
    flash(2)
    gather.second_far(0)
    flash(3)
    flash(4)
    gather.second_near(2)
    gather.second_far(3)
    flash(5)
    flash(6)
    gather.second_far(1)
    gather.second_far(2)
    for pair, k, j in ARRIVAL[28:]:
        if pair:
            gather.from_sibling(k, j)

    partner = (tp + 2) % 4
    sibling = (x, s, tp + 1 - 2 * core)
    mine = x % 2 == core
    spans = [pl.ds(0, 3 * HD), pl.ds(3 * HD, 2 * HD)]

    def swap(g):
        return remote(attn.at[:, spans[g]], pair_attn.at[:, spans[g]], y_send.at[g], y_recv.at[g], (x, s, partner))

    def near(i, g):
        held = (attn, pair_attn)[i]
        return pltpu.make_async_copy(held.at[:, spans[g]], afull.at[x, :, spans[g]], local_sem.at[2 + 2 * i + g])

    def away(i, g, plane):
        held = (attn, pair_attn)[i]
        return remote(
            held.at[:, spans[g]], afull.at[plane, :, spans[g]], a_send.at[2 * i + g], a_recv.at[2 * plane + g],
            ((tp, partner)[i], s, tp),
        )

    def deliver(i, g):
        block = (tp, partner)[i]

        @pl.when(x == block)
        def _():
            near(i, g).start()

        @pl.when(x != block)
        def _():
            away(i, g, x).start()

    def pair_copy(g, d):
        ref = afull.at[(x + d) % 4, :, spans[g]]
        return remote(ref, ref, a_pair_send.at[4 * g + d], a_pair_recv.at[4 * g + d], sibling)

    def collect(g, d):
        @pl.when(mine)
        def _():
            if d == 0:
                @pl.when(x == tp)
                def _():
                    near(0, g).wait()

                @pl.when(x != tp)
                def _():
                    near(1, g).wait()
            else:
                away(0, g, (x + d) % 4).wait_recv()
            pair_copy(g, d).start()

        @pl.when(jnp.logical_not(mine))
        def _():
            pair_copy(g, d).wait_recv()

    def last(h, carry):
        step(h, 7)
        total = jnp.sum(low[h], axis=1, keepdims=True)
        attn[:, pl.ds(pl.multiple_of(h * HD, HD), HD)] = (acc[h] / total).astype(jnp.bfloat16)

        @pl.when(h == 3)
        def _():
            swap(0).start()
            deliver(0, 0)

        return carry

    lax.fori_loop(0, HEADS_HERE, last, 0)
    need_wo()
    swap(1).start()
    deliver(0, 1)
    swap(0).wait_recv()
    deliver(1, 0)

    def project(g, d):
        plane = (x + d) % 4
        first, count = ((0, 3 * HD), (3 * HD, 2 * HD))[g]
        return jnp.dot(
            afull[plane, :, first : first + count], wofull[plane, first : first + count, :],
            preferred_element_type=jnp.float32,
        )

    swap(1).wait_recv()
    deliver(1, 1)
    for d in (0, 1, 3, 2):
        collect(0, d)
        if d == 0:
            proj[...] = project(0, d)
        else:
            proj[...] += project(0, d)
    for d in (0, 1, 3, 2):
        collect(1, d)
        proj[...] += project(1, d)

    own_inputs.wait()
    own_gate.wait()
    block = (inputs_ref[...].astype(jnp.float32) + gate_ref[2:3] * proj[...]).astype(jnp.bfloat16)
    block_out[...] = block
    differ = block.astype(jnp.float32) - policy_ref[...].astype(jnp.float32)
    errs[0] = to_row(jnp.sum(differ * differ, axis=1, keepdims=True))
    for i in range(2):
        for g in range(2):
            @pl.when(x != (tp, partner)[i])
            def _(i=i, g=g):
                away(i, g, x).wait_send()
    for g in range(2):
        swap(g).wait_send()

    @pl.when(mine)
    def _():
        for g in range(2):
            for d in range(4):
                pair_copy(g, d).wait_send()

    shares = [remote(errs.at[0], errs.at[d], e_send.at[d], e_recv.at[d], (x, s, (tp + d) % 4)) for d in (1, 2, 3)]
    for share in shares:
        share.start()
    for copy in own_sends + onward:
        copy.wait_send()
    gather.finish()
    for share in shares:
        share.wait()
    err_out[...] = ((errs[0] + errs[1]) + (errs[2] + errs[3])) / D


def attend_call(q, kv, wo, x, policy, mod):
    return pl.pallas_call(
        attend_kernel,
        out_shape=[
            jax.ShapeDtypeStruct((ROWS, D // 4), jnp.bfloat16),
            jax.ShapeDtypeStruct((8, ROWS), jnp.float32),
        ],
        in_specs=[VMEM, ANY, ANY, ANY, VMEM, ANY],
        out_specs=[VMEM, VMEM],
        scratch_shapes=[
            pltpu.VMEM((ROWS, D // 4), jnp.bfloat16),
            pltpu.VMEM((8, D // 4), jnp.float32),
            pltpu.VMEM((32, ROWS, 2 * COLS), jnp.bfloat16),
            pltpu.VMEM((4, COLS, 2 * COLS), jnp.bfloat16),
            pltpu.VMEM((HEADS_HERE, ROWS, HD), jnp.float32),
            pltpu.VMEM((HEADS_HERE, ROWS, HD), jnp.float32),
            pltpu.VMEM((HEADS_HERE, ROWS, HD), jnp.float32),
            pltpu.VMEM((ROWS, COLS), jnp.bfloat16),
            pltpu.VMEM((ROWS, COLS), jnp.bfloat16),
            pltpu.VMEM((4, ROWS, COLS), jnp.bfloat16),
            pltpu.VMEM((ROWS, D // 4), jnp.float32),
            pltpu.VMEM((4, 8, ROWS), jnp.float32),
            *gather_sems(1),
            pltpu.SemaphoreType.DMA((6,)),
            pltpu.SemaphoreType.DMA((6,)),
            pltpu.SemaphoreType.DMA((8,)),
            pltpu.SemaphoreType.DMA((4,)),
            pltpu.SemaphoreType.DMA((8,)),
            pltpu.SemaphoreType.DMA((8,)),
            pltpu.SemaphoreType.DMA((8,)),
            pltpu.SemaphoreType.DMA((2,)),
            pltpu.SemaphoreType.DMA((2,)),
            pltpu.SemaphoreType.DMA((4,)),
            pltpu.SemaphoreType.DMA((4,)),
        ],
        compiler_params=pltpu.CompilerParams(has_side_effects=True, vmem_limit_bytes=LIMIT, collective_id=5),
        name="attend",
    )(q, kv, wo, x, policy, mod)


def local(latents, policy_out, w_qkv, w_out, qk_gains, mod_table, timestep, owner):
    held = w_qkv.shape[0]
    local_block = owner[0] % held
    root_group = owner[0] // held
    mine_qkv = lax.dynamic_index_in_dim(w_qkv.transpose(0, 2, 1, 3), local_block, 0, keepdims=False)
    mine_out = lax.dynamic_index_in_dim(w_out, local_block, 0, keepdims=False)
    mine_gains = lax.dynamic_index_in_dim(qk_gains, local_block, 0, keepdims=False)
    mine_gains = jnp.pad(mine_gains, ((0, 14), (0, 0)))
    onehot = (jnp.arange(mod_table.shape[0], dtype=jnp.int32) == timestep[0]).astype(jnp.float32)
    modulation = jnp.tensordot(onehot, mod_table, axes=1, precision=lax.Precision.HIGHEST)
    mod = jnp.pad(modulation, ((0, 5), (0, 0)))
    q, kv, wo_rows = lax.switch(
        root_group,
        [lambda *a, root=root: tuple(qkv_call(root, *a)) for root in range(4)],
        mine_qkv, mine_out, mine_gains, latents[0], mod,
    )
    block, squares = attend_call(q, kv, wo_rows, latents[0], policy_out[0], mod)
    return (block[None], squares[0:1])


def solution(mesh):
    placed = (
        P(None, ("own", "seq"), None),
        P(None, ("own", "seq"), "tp"),
        P("own", "seq", None, "tp"),
        P("own", "tp", "seq"),
        P("own", None, "tp"),
        P(),
        P(),
        P(),
    )
    return jax.shard_map(
        local,
        mesh=mesh,
        in_specs=placed,
        out_specs=(P(None, ("own", "seq"), "tp"), P(None, ("own", "seq"))),
        check_vma=False,
    )
```
